256 devices in a mesh: lvl: 4 (over x), gx: 16 (over z_hi, y), gy: 4 (over z_lo, core).
Axes of the slice: x: 4, y: 4, z: 8 (z_hi: 4, z_lo: 2; z = z_hi * 2 + z_lo), core: 2. Of those that a mesh axis runs over, the one named last changes fastest.
Arguments:
- initial: float32 [16, 128, 32, 128], P(None, 'gx', 'gy'), may hold values from 0.07 to 1, as said below
- rate_factor: float32 [128, 32, 128], P('gx', 'gy'), may hold values from 0.5 to 2
- diffusivity: float32 [16], replicated, may hold values from 0.3 to 2
- loss_rate: float32 [16], replicated, may hold values from 0.05 to 1.5
- quench: float32 [16, 16], replicated, may hold values from 0 to 0.1
- formation: float32 [16, 16], replicated, may hold values from 0 to 0.1
Outputs:
- final: float32 [4, 16, 128, 32, 128], P('lvl', None, 'gx', 'gy')
The draws below stay inside these ranges and needn't reach their ends.
Inputs may be any that keep to these rules, and one draw needn't show every extreme that they name: `initial`: positive concentrations.
All inputs are finite; a program needn't handle non-finite values.
Results may differ from the reference program's by a relative error of at most 0.0001.
Values sent between devices are 32-bit elements; how exact they have to be, the bound alone decides.
A program may use at most 64 MiB of HBM per device.

```python
import math
import jax
import jax.numpy as jnp
from jax import lax

C = 16
REACT = 11
NZ = 128
STEPS = 4
SWEEPS = 4
NX = 128
NY = 32
N_LVL = 4


def draw_initial(key, part):
    baseline = jnp.exp(jax.random.uniform(key, (C, NX, NY, NZ), jnp.float32, math.log(0.1), math.log(1.0)))
    return baseline


def steps_of(stream_key, dims, cuts, least, top_value):
    def one(dim, parts):
        heights = jax.random.uniform(jax.random.fold_in(jax.random.fold_in(stream_key, 6), dim), (parts,), jnp.float32, least / len(cuts), top_value / len(cuts))
        return jnp.repeat(jnp.exp(heights), dims[dim] // parts).reshape((-1,) + (1,) * (len(dims) - dim - 1))

    factor_of = one(*cuts[0])
    for cut in cuts[1:]:
        factor_of = factor_of * one(*cut)
    return factor_of


def setup_inputs(seed: int = 0) -> dict:
    key_list = jax.random.split(jax.random.key(seed), 7)
    initial = draw_initial(jax.random.fold_in(key_list[6], 71), 0)
    rate_factor = jnp.clip(jnp.exp(math.log(2.0) - 1.3862944 * jax.random.uniform(key_list[1], (NX, NY, NZ), jnp.float32) ** steps_of(key_list[1], (NX, NY, NZ), ((0, 16), (1, 4)), -0.2, 0.2)), 0.5, 2.0)
    diffusivity = jnp.clip(jnp.exp(jax.random.uniform(key_list[2], (C,), jnp.float32, math.log(0.3), math.log(2.0))), 0.3, 2.0)
    loss_rate = jnp.clip(jnp.exp(jax.random.uniform(key_list[3], (C,), jnp.float32, math.log(0.05), math.log(1.5))), 0.05, 1.5)
    quench = jnp.clip(jax.random.uniform(key_list[4], (C, C), jnp.float32, 0.0, 0.1), 0.0, 0.1)
    formation = jnp.clip(jax.random.uniform(key_list[5], (C, C), jnp.float32, 0.0, 0.1), 0.0, 0.1)
    return {"initial": initial, "rate_factor": rate_factor, "diffusivity": diffusivity, "loss_rate": loss_rate, "quench": quench, "formation": formation}


def pad_rim(values):
    return jnp.pad(values, ((0, 0), (1, 1), (1, 1), (0, 0)))


def conduct(fields, diffusivity):
    return diffusivity[:, None, None, None] * (1.0 + fields * fields)


def face_weights(padded, diffusivity):
    conductance = conduct(padded, diffusivity)
    centre = conductance[:, 1:-1, 1:-1]
    inner_cells = padded[:, 1:-1, 1:-1]
    vertical = conduct(jnp.pad(inner_cells, ((0, 0), (0, 0), (0, 0), (1, 1))), diffusivity)
    west_face = 0.5 * (centre + conductance[:, :-2, 1:-1])
    east_face = 0.5 * (centre + conductance[:, 2:, 1:-1])
    south_face = 0.5 * (centre + conductance[:, 1:-1, :-2])
    north_face = 0.5 * (centre + conductance[:, 1:-1, 2:])
    lower_face = 0.5 * (centre + vertical[..., :-2])
    upper_face = 0.5 * (centre + vertical[..., 2:])
    weight_sum = west_face + east_face + south_face + north_face + lower_face + upper_face
    return (west_face, east_face, south_face, north_face, lower_face, upper_face), weight_sum


def neighbours(padded, coeffs):
    west_face, east_face, south_face, north_face, lower_face, upper_face = coeffs
    inner_cells = padded[:, 1:-1, 1:-1]
    stacked = jnp.pad(inner_cells, ((0, 0), (0, 0), (0, 0), (1, 1)))
    return (west_face * padded[:, :-2, 1:-1] + east_face * padded[:, 2:, 1:-1]
            + south_face * padded[:, 1:-1, :-2] + north_face * padded[:, 1:-1, 2:]
            + lower_face * stacked[..., :-2] + upper_face * stacked[..., 2:])


def chemistry(fields, rate_factor, loss_rate, quench, formation):
    reacting = (jnp.arange(fields.shape[0]) < REACT).astype(jnp.float32)[:, None, None, None]
    squares = jnp.einsum("ij,jxyz->ixyz", quench, fields * fields, precision=lax.Precision.HIGHEST)
    produced = jnp.einsum("ij,jxyz->ixyz", formation, fields, precision=lax.Precision.HIGHEST)
    loss_term = reacting * loss_rate[:, None, None, None] * rate_factor[None] * (1.0 + squares)
    production = reacting * rate_factor[None] * produced
    return loss_term, production


def reference(initial, rate_factor, diffusivity, loss_rate, quench, formation):
    inflows = [jnp.zeros_like(initial) for step_index in range(STEPS)]
    finals = []
    for level_index in range(N_LVL):
        current_state = initial
        outgoing = []
        previous_tendency = jnp.zeros_like(initial)
        carried = jnp.zeros_like(initial)
        for node_index in range(STEPS + 1):
            padded = pad_rim(current_state)
            coeffs, weight_sum = face_weights(padded, diffusivity)
            loss_term, production = chemistry(current_state, rate_factor, loss_rate, quench, formation)
            diffused = neighbours(padded, coeffs) - weight_sum * current_state
            tendency = diffused + production - loss_term * current_state
            if node_index > 0:
                outgoing.append(0.5 * (previous_tendency + tendency) - carried)
            if node_index < STEPS:
                right_side = current_state + production + inflows[node_index]
                denominator = 1.0 + loss_term + weight_sum
                iterate = current_state
                padded_now = padded
                for sweep_index in range(SWEEPS):
                    if sweep_index > 0:
                        padded_now = pad_rim(iterate)
                    iterate = (right_side + neighbours(padded_now, coeffs)) / denominator
                carried = production + (iterate - right_side)
                previous_tendency = tendency
                current_state = iterate
        finals.append(current_state)
        inflows = outgoing
    return jnp.stack(finals)
```

```python
import functools

import jax
import jax.numpy as jnp
from jax import lax
from jax.experimental import pallas as pl
from jax.experimental.pallas import tpu as pltpu
from jax.sharding import PartitionSpec as P

MESH = pl.DeviceIdType.MESH
REACT = 11
STEPS = 4
LEVELS = 4
C = 16
NZ = 128
T = 4
W = 2
E = T + 2 * W
DIRS = ((1, 0), (-1, 0), (0, 1), (0, -1), (1, 1), (-1, -1), (1, -1), (-1, 1))


def spans(d):
    if d == 1:
        return W + T - W, 0, W
    if d == -1:
        return W, W + T, W
    return W, W, T


def corner_spans(d):
    return (W + T - 1, W - 1, 1) if d == 1 else (W, W + T, 1)


def box(dx, dy):
    if dx and dy:
        return corner_spans(dx), corner_spans(dy)
    return spans(dx), spans(dy)


def here():
    lvl, gx, gy = lax.axis_index("lvl"), lax.axis_index("gx"), lax.axis_index("gy")
    lx, ly = lvl // 2, (lvl + lvl // 2) % 2
    return 2 * gx + (lx + gx) % 2, 2 * gy + (ly + gy) % 2


def device_at(X, Y):
    gx, gy = X // 2, Y // 2
    lx, ly = (X % 2 + gx) % 2, (Y % 2 + gy) % 2
    return lx * (3 - 2 * ly) + ly, gx, gy


def kernel(nx, ny, ini, rf, dh_ref, lr_ref, wq_ref, wf_ref, out,
           stage, U, V2, V1, K, WX, WY, WZ, RHS, INV, ACC, INF, PQ, RF,
           i_send, i_recv, u_send, u_recv, v_send, v_recv, f_send, f_recv):
    lvl, gx, gy = lax.axis_index("lvl"), lax.axis_index("gx"), lax.axis_index("gy")
    X, Y = here()

    def exists(dx, dy):
        ok = None
        for d, at, n in ((dx, X, nx), (dy, Y, ny)):
            if d:
                c = at < n - 1 if d == 1 else at > 0
                ok = c if ok is None else ok & c
        return ok

    def each(f):
        for i, (dx, dy) in enumerate(DIRS):
            @pl.when(exists(dx, dy))
            def _():
                f(i, dx, dy)

    S0 = stage.at[1]
    zero = jnp.zeros((E, 24, NZ), jnp.float32)
    zero_v = jnp.zeros((E, C, NZ), jnp.float32)

    def clear(x, c):
        S0[x] = zero
        for p in range(LEVELS):
            V2[p, x] = zero_v
        return c

    lax.fori_loop(0, E, clear, 0)

    nat = stage.at[0]
    for x in range(8):
        nat[x, :, 0:C, :] = jnp.swapaxes(ini[:, x], 0, 1)
        nat[x, :, C:24, :] = jnp.broadcast_to(rf[x][:, None, :], (8, 8, NZ))

    bar = pltpu.get_barrier_semaphore()

    def greet(device):
        pl.semaphore_signal(bar, inc=1, device_id=device, device_id_type=MESH)

    each(lambda i, dx, dy: greet(device_at(X + dx, Y + dy)))
    for k in range(1, LEVELS):
        greet(((lvl + k) % LEVELS, gx, gy))
    beside = sum(exists(dx, dy).astype(jnp.int32) for dx, dy in DIRS)
    pl.semaphore_wait(bar, beside + LEVELS - 1)

    ox, oy = T * (X % 2), T * (Y % 2)

    def init_copy(i, dx, dy, device):
        (sx, tx, mx), (sy, ty, my) = box(dx, dy)
        return pltpu.make_async_remote_copy(
            src_ref=nat.at[pl.ds(ox + sx - W, mx), pl.ds(oy + sy - W, my)],
            dst_ref=S0.at[tx:tx + mx, ty:ty + my],
            send_sem=i_send.at[i], recv_sem=i_recv.at[i], device_id=device, device_id_type=MESH)

    each(lambda i, dx, dy: init_copy(i, dx, dy, device_at(X + dx, Y + dy)).start())
    for x in range(T):
        S0[W + x, W:W + T] = nat[ox + x, pl.ds(oy, T)]
    each(lambda i, dx, dy: init_copy(i ^ 1, -dx, -dy, device_at(X + dx, Y + dy)).wait_recv())
    for x in range(E):
        for h in range(2):
            RF[x, :, 8 * h:8 * h + 8, :] = S0[x, :, C:24, :]
    each(lambda i, dx, dy: init_copy(i, dx, dy, device_at(X + dx, Y + dy)).wait_send())

    def rim_copy(buf, send, recv, p, i, dx, dy, device):
        (sx, tx, mx), (sy, ty, my) = box(dx, dy)
        return pltpu.make_async_remote_copy(
            src_ref=buf.at[p, sx:sx + mx, sy:sy + my],
            dst_ref=buf.at[p, tx:tx + mx, ty:ty + my],
            send_sem=send.at[p, i], recv_sem=recv.at[p, i], device_id=device, device_id_type=MESH)

    def rim_start(buf, send, recv, p):
        each(lambda i, dx, dy: rim_copy(buf, send, recv, p, i, dx, dy, device_at(X + dx, Y + dy)).start())

    def rim_wait(buf, send, recv, p):
        each(lambda i, dx, dy: rim_copy(buf, send, recv, p, i ^ 1, -dx, -dy, device_at(X + dx, Y + dy)).wait_recv())
        each(lambda i, dx, dy: rim_copy(buf, send, recv, p, i, dx, dy, device_at(X + dx, Y + dy)).wait_send())

    def final_copy(p):
        return pltpu.make_async_remote_copy(
            src_ref=U.at[p, W:W + T, W:W + T],
            dst_ref=out.at[pl.ds(ox, T), pl.ds(oy, T)],
            send_sem=f_send.at[p], recv_sem=f_recv.at[lvl], device_id=(p, gx, gy), device_id_type=MESH)

    lane = lax.broadcasted_iota(jnp.int32, (1, C, NZ), 2)
    first, last = lane == 0, lane == NZ - 1
    R = [(W, W + T) if x in (W - 1, W + T) else (W - 1, W + T + 1) for x in range(E)]

    def up(v):
        return pltpu.roll(v, 1, 2)

    def down(v):
        return pltpu.roll(v, NZ - 1, 2)

    def sweep(p, src, dst, rows, cols):
        for x in rows:
            lo, hi = cols(x)
            for a in range(lo, hi, 2):
                b = min(a + 2, hi)
                c = src(x, a - 1, b + 1)
                v, wz = c[1:-1], WZ[p, x, a:b]
                wy = WY[p, x, a - 1:b]
                n = (WX[p, x - 1, a:b] * src(x - 1, a, b) + WX[p, x, a:b] * src(x + 1, a, b)
                     + wy[:-1] * c[:-2] + wy[1:] * c[2:] + wz * up(v) + down(wz * v))
                dst(x, a, b, (RHS[p, x, a:b] + n) * INV[p, x, a:b])

    def split(u):
        hi = u.astype(jnp.bfloat16)
        lo = (u - hi.astype(jnp.float32)).astype(jnp.bfloat16)
        return jnp.concatenate([hi, lo, hi], axis=0)

    def chemistry(p):
        def one(get, put):
            u = get().reshape(4 * C, NZ)
            for k, w_ref, v in ((0, wf_ref, u), (1, wq_ref, u * u)):
                put(k, jnp.dot(w_ref[...], split(v), preferred_element_type=jnp.float32).reshape(4, C, NZ))

        for x in range(W - 1, W + T + 1):
            def put(k, v, x=x):
                PQ[k, x, W:W + T] = v
            one(lambda: U[p, x, W:W + T], put)
        for y in (W - 1, W + T):
            def put(k, v, y=y):
                for x in range(T):
                    PQ[k, W + x, y] = v[x]
            one(lambda: U[p, W:W + T, y], put)

    def setup(p):
        dh = dh_ref[...][None]
        lr = lr_ref[...][None]
        for x in range(E):
            lo, hi = (W, W + T) if x in (0, E - 1) else (R[x] if x in (1, E - 2) else (0, E))
            if x in (1, E - 2):
                lo, hi = 1, E - 1
            for a in range(lo, hi, 2):
                u = U[p, x, a:a + 2]
                K[x, a:a + 2] = dh + dh * (u * u)
        chemistry(p)
        for x in range(W - 1, W + T + 1):
            lo, hi = R[x]
            for a in range(lo, hi, 2):
                b = a + 2
                kc = K[x, a - 1:b + 1]
                k = kc[1:-1]
                kw, ke = K[x - 1, a:b], K[x + 1, a:b]
                ww, we, ws, wn = k + kw, k + ke, k + kc[:-2], k + kc[2:]
                kl = jnp.where(first, dh, up(k))
                kh = jnp.where(last, dh, down(k))
                wl = k + kl
                total = ((ww + we) + (ws + wn)) + (wl + (k + kh))
                wz = jnp.where(first, 0.0, wl)
                if x <= W + T - 1:
                    WX[p, x - 1, a:b] = ww
                if x >= W + T - 1:
                    WX[p, x, a:b] = we
                WY[p, x, a - 1:b - 1] = ws
                if b == hi:
                    WY[p, x, b - 1:b] = wn[-1:]
                WZ[p, x, a:b] = wz
                uc = U[p, x, a - 1:b + 1]
                u = uc[1:-1]
                n = (ww * U[p, x - 1, a:b] + we * U[p, x + 1, a:b] + ws * uc[:-2] + wn * uc[2:]
                     + wz * up(u) + down(wz * u))
                r = RF[x, a:b]
                made = r * PQ[0, x, a:b]
                lost = total + r * (lr + PQ[1, x, a:b])
                half = 0.5 * ((n + made) - lost * u)
                inv = 1.0 / (1.0 + lost)
                inflow = INF[x, a:b]
                old = ACC[p, x, a:b]
                right = (u + made) + inflow
                INF[x, a:b] = (old + half) - u
                ACC[p, x, a:b] = (half + u) + inflow
                RHS[p, x, a:b] = right
                INV[p, x, a:b] = inv
                V1[x, a:b] = (right + n) * inv

    none_v = jnp.zeros((1, C, NZ), jnp.float32)

    def mask(p):
        for cond, cells in ((X == 0, [(W - 1, y) for y in range(W, W + T)]),
                            (X == nx - 1, [(W + T, y) for y in range(W, W + T)]),
                            (Y == 0, [(x, W - 1) for x in range(W, W + T)]),
                            (Y == ny - 1, [(x, W + T) for x in range(W, W + T)])):
            @pl.when(cond)
            def _():
                for x, y in cells:
                    V1[x, y:y + 1] = none_v
                    INV[p, x, y:y + 1] = none_v

    inner = range(W, W + T)
    outer = range(W - 1, W + T + 1)

    def store_v1(x, a, b, v):
        V1[x, a:b] = v

    def phase_a(t, p):
        n = t - p

        @pl.when((n >= 0) & ((n < STEPS) | ((n == STEPS) & (p < LEVELS - 1))))
        def _():
            @pl.when(n == 0)
            def _():
                for x in range(E):
                    U[p, x] = S0[x, :, 0:C, :]

            @pl.when(n > 0)
            def _():
                rim_wait(U, u_send, u_recv, p)

            setup(p)

            @pl.when(n < STEPS)
            def _():
                mask(p)

                def put(x, a, b, v):
                    V2[p, x, a:b] = v
                sweep(p, lambda x, a, b: V1[x, a:b], put, inner, lambda x: (W, W + T))
                rim_start(V2, v_send, v_recv, p)

    def phase_b(t, p):
        n = t - p

        @pl.when((n >= 0) & (n < STEPS))
        def _():
            rim_wait(V2, v_send, v_recv, p)
            sweep(p, lambda x, a, b: V2[p, x, a:b], store_v1, outer, lambda x: R[x])

            def put(x, a, b, v):
                U[p, x, a:b] = v
            sweep(p, lambda x, a, b: V1[x, a:b], put, inner, lambda x: (W, W + T))

            @pl.when((n < STEPS - 1) | (p < LEVELS - 1))
            def _():
                rim_start(U, u_send, u_recv, p)

            @pl.when(n == STEPS - 1)
            def _():
                @pl.when(p != lvl)
                def _():
                    final_copy(p).start()

                @pl.when(p == lvl)
                def _():
                    for x in range(T):
                        out[ox + x, pl.ds(oy, T)] = U[p, W + x, W:W + T]

    def tick(t, c):
        for x in range(1, E - 1):
            INF[x] = zero_v
        lax.fori_loop(0, LEVELS, lambda p, c: (phase_a(t, p), c)[1], 0)
        lax.fori_loop(0, LEVELS, lambda p, c: (phase_b(t, p), c)[1], 0)
        return c

    lax.fori_loop(0, STEPS + LEVELS - 1, tick, 0)

    for k in range(1, LEVELS):
        src = (lvl + k) % LEVELS
        pltpu.make_async_remote_copy(
            src_ref=U.at[0, W:W + T, W:W + T], dst_ref=out.at[0:T, 0:T],
            send_sem=f_send.at[0], recv_sem=f_recv.at[src], device_id=(src, gx, gy), device_id_type=MESH).wait_recv()
    for p in range(LEVELS):
        @pl.when(p != lvl)
        def _():
            final_copy(p).wait_send()


def on_device(nx, ny, initial, rate_factor, diffusivity, loss_rate, quench, formation):
    def rows(v):
        return jnp.broadcast_to(v[:, None], (C, NZ))

    reacting = jnp.arange(C) < REACT
    lr = jnp.where(reacting, loss_rate, 0.0)
    wide = jnp.eye(4, dtype=jnp.float32)

    def blocks(m):
        m = jnp.where(reacting[:, None], m, 0.0)
        big = (wide[:, None, :, None] * m[None, :, None, :]).reshape(4 * C, 4 * C)
        hi = lax.reduce_precision(big, 8, 7)
        lo = (big - hi).astype(jnp.bfloat16)
        hi = hi.astype(jnp.bfloat16)
        return jnp.concatenate([hi, hi, lo], axis=1)

    f32 = jnp.float32
    frame = (E, E, C, NZ)
    vmem = pl.BlockSpec(memory_space=pltpu.VMEM)
    dma = pltpu.SemaphoreType.DMA
    done = pl.pallas_call(
        functools.partial(kernel, nx, ny),
        name="deferred_correction",
        out_shape=jax.ShapeDtypeStruct((8, 8, C, NZ), f32),
        in_specs=[vmem] * 6,
        out_specs=vmem,
        scratch_shapes=[
            pltpu.VMEM((2, E, E, 24, NZ), f32),
            pltpu.VMEM((LEVELS,) + frame, f32),
            pltpu.VMEM((LEVELS,) + frame, f32),
            pltpu.VMEM(frame, f32),
            pltpu.VMEM(frame, f32),
            pltpu.VMEM((LEVELS,) + frame, f32),
            pltpu.VMEM((LEVELS,) + frame, f32),
            pltpu.VMEM((LEVELS,) + frame, f32),
            pltpu.VMEM((LEVELS,) + frame, f32),
            pltpu.VMEM((LEVELS,) + frame, f32),
            pltpu.VMEM((LEVELS,) + frame, f32),
            pltpu.VMEM(frame, f32),
            pltpu.VMEM((2,) + frame, f32),
            pltpu.VMEM(frame, f32),
            dma((8,)), dma((8,)),
            dma((LEVELS, 8)), dma((LEVELS, 8)),
            dma((LEVELS, 8)), dma((LEVELS, 8)),
            dma((LEVELS,)), dma((LEVELS,)),
        ],
        compiler_params=pltpu.CompilerParams(
            collective_id=0, has_side_effects=True, vmem_limit_bytes=44 << 20),
    )(initial, rate_factor, rows(0.5 * diffusivity), rows(lr), blocks(loss_rate[:, None] * quench), blocks(formation))
    return done.transpose(2, 0, 1, 3)[None]


def solution(mesh):
    in_specs = (P(None, "gx", "gy", None), P("gx", "gy", None), P(), P(), P(), P())
    out_specs = P("lvl", None, "gx", "gy", None)
    nx, ny = 2 * mesh.shape["gx"], 2 * mesh.shape["gy"]
    return jax.shard_map(
        functools.partial(on_device, nx, ny), mesh=mesh, in_specs=in_specs, out_specs=out_specs, check_vma=False)
```

```python
import functools

import jax
import jax.numpy as jnp
from jax import lax
from jax.experimental import pallas as pl
from jax.experimental.pallas import tpu as pltpu
from jax.sharding import PartitionSpec as P

MESH = pl.DeviceIdType.MESH
REACT = 11
STEPS = 4
LEVELS = 4
C = 16
NZ = 128
T = 4
W = 2
E = T + 2 * W
DIRS = ((1, 0), (-1, 0), (0, 1), (0, -1), (1, 1), (-1, -1), (1, -1), (-1, 1))


def spans(d):
    if d == 1:
        return W + T - W, 0, W
    if d == -1:
        return W, W + T, W
    return W, W, T


def corner_spans(d):
    return (W + T - 1, W - 1, 1) if d == 1 else (W, W + T, 1)


def box(dx, dy):
    if dx and dy:
        return corner_spans(dx), corner_spans(dy)
    return spans(dx), spans(dy)


def here():
    lvl, gx, gy = lax.axis_index("lvl"), lax.axis_index("gx"), lax.axis_index("gy")
    y = gx % 4
    back = y // 2
    m = (y + back) % 2
    strip = 4 * (gx // 4) + m + (gy // 2) * (3 - 2 * m)
    return 2 * strip + gy % 2, lvl + back * (7 - 2 * lvl)


def device_at(X, Y):
    strip, back, r = X // 2, Y // 4, Y % 4
    s = strip % 4
    m = (s + s // 2) % 2
    y = m + back * (3 - 2 * m)
    return r + back * (3 - 2 * r), 4 * (strip // 4) + y, 2 * (s // 2) + X % 2


def kernel(nx, ny, ini, rf, d_ref, l_ref, quench_ref, formation_ref, out,
           stage, U, V2, V1, K, WX, WY, WZ, RHS, INV, ACC, INF, PQ, RF, flat, flat24,
           dh_ref, lr_ref, wq_ref, wf_ref, G,
           i_send, i_recv, u_send, u_recv, v_send, v_recv, g_send, g_recv, f_send, f_recv):
    lvl, gx, gy = lax.axis_index("lvl"), lax.axis_index("gx"), lax.axis_index("gy")
    me = (lvl, gx, gy)
    X, Y = here()

    def other(device):
        return (device[0] != lvl) | (device[1] != gx) | (device[2] != gy)

    def exists(dx, dy):
        ok = None
        for d, at, n in ((dx, X, nx), (dy, Y, ny)):
            if d:
                c = at < n - 1 if d == 1 else at > 0
                ok = c if ok is None else ok & c
        return ok

    beside = [(exists(dx, dy), device_at(X + dx, Y + dy)) for dx, dy in DIRS]
    gives = lvl // 2 == (gy + gy // 2) % 2
    YA = lvl + (gy // 2) * (7 - 2 * lvl)
    takers = [device_at(2 * gx + e, YA) for e in range(2)]
    giver = (lvl, X // 2, Y // 2)
    row_of_four = [((lvl + k) % LEVELS, gx, gy) for k in range(1, LEVELS)]

    def each(f):
        for i, (dx, dy) in enumerate(DIRS):
            @pl.when(beside[i][0])
            def _():
                f(i, dx, dy, beside[i][1])

    S0 = stage.at[1]
    zero = jnp.zeros((E, 24, NZ), jnp.float32)
    zero_v = jnp.zeros((E, C, NZ), jnp.float32)

    edge_x, edge_y = (X == 0) | (X == nx - 1), (Y == 0) | (Y == ny - 1)

    def clear(x, c):
        S0[x] = zero
        for p in range(LEVELS):
            V2[p, x] = zero_v
        return c

    @pl.when(edge_x | edge_y)
    def _():
        lax.fori_loop(0, E, clear, 0)

    bar = pltpu.get_barrier_semaphore()

    def greet(device):
        pl.semaphore_signal(bar, inc=1, device_id=device, device_id_type=MESH)

    each(lambda i, dx, dy, device: greet(device))
    others = [(lvl >= 0, device) for device in row_of_four]
    others += [(gives & other(device), device) for device in takers] + [(other(giver), giver)]
    for cond, device in others:
        @pl.when(cond)
        def _():
            greet(device)

    reacts = lax.broadcasted_iota(jnp.int32, (C, NZ), 0) < REACT
    dh_ref[...] = jnp.broadcast_to(0.5 * d_ref[...], (C, NZ))
    lr_ref[...] = jnp.where(reacts, jnp.broadcast_to(l_ref[...], (C, NZ)), 0.0)
    row, col = (lax.broadcasted_iota(jnp.int32, (4 * C, 4 * C), k) for k in range(2))
    for w_ref, m in ((wq_ref, quench_ref[...] * l_ref[...]), (wf_ref, formation_ref[...])):
        m = jnp.concatenate([jnp.concatenate([m] * 4, axis=1)] * 4, axis=0)
        m = jnp.where((row // C == col // C) & (row % C < REACT), m, 0.0)
        hi = m.astype(jnp.bfloat16).astype(jnp.float32)
        w_ref[...] = jnp.concatenate([hi, hi, m - hi], axis=1).astype(jnp.bfloat16)

    nat = stage.at[0]
    for x in range(8):
        nat[x, :, 0:C, :] = jnp.swapaxes(ini[:, x], 0, 1)
        nat[x, :, C:24, :] = jnp.broadcast_to(rf[x][:, None, :], (8, 8, NZ))

    count = sum(ok.astype(jnp.int32) for ok, _ in beside) + sum(cond.astype(jnp.int32) for cond, _ in others)
    pl.semaphore_wait(bar, count)

    def hand(e, device):
        return pltpu.make_async_remote_copy(
            src_ref=nat.at[T * e:T * e + T, pl.ds(T * (YA % 2), T)],
            dst_ref=S0.at[W:W + T, W:W + T],
            send_sem=i_send.at[1 + e], recv_sem=i_recv.at[1], device_id=device, device_id_type=MESH)

    for e, device in enumerate(takers):
        @pl.when(gives & other(device))
        def _():
            hand(e, device).start()

        @pl.when(gives & jnp.logical_not(other(device)))
        def _():
            for x in range(T):
                S0[W + x, W:W + T] = nat[T * e + x, pl.ds(T * (YA % 2), T)]

    @pl.when(other(giver))
    def _():
        hand(0, giver).wait_recv()

    def rim_copy(ref, send, recv, dx, dy, device):
        (sx, tx, mx), (sy, ty, my) = box(dx, dy)
        return pltpu.make_async_remote_copy(
            src_ref=ref.at[sx:sx + mx, sy:sy + my], dst_ref=ref.at[tx:tx + mx, ty:ty + my],
            send_sem=send, recv_sem=recv, device_id=device, device_id_type=MESH)

    inside = jnp.logical_not(edge_x | edge_y)
    at_corner = edge_x & edge_y
    at_edge = (edge_x | edge_y) & jnp.logical_not(at_corner)

    def rim_wait_for(ref, send, recv):
        for cond, cells in ((inside, 8 * W + 8 * W + 4), (at_edge, 12 * W + 2), (at_corner, 8 * W + 1)):
            @pl.when(cond)
            def _():
                copy = pltpu.make_async_remote_copy(
                    src_ref=ref.at[0:cells], dst_ref=ref.at[0:cells],
                    send_sem=send, recv_sem=recv, device_id=me, device_id_type=MESH)
                copy.wait_recv()
                copy.wait_send()

    each(lambda i, dx, dy, device: rim_copy(S0, i_send.at[0], i_recv.at[0], dx, dy, device).start())
    rim_wait_for(flat24, i_send.at[0], i_recv.at[0])
    for x in range(E):
        for h in range(2):
            RF[x, :, 8 * h:8 * h + 8, :] = S0[x, :, C:24, :]

    def rim_start(buf, send, recv, p):
        each(lambda i, dx, dy, device: rim_copy(buf.at[p], send.at[p], recv.at[p], dx, dy, device).start())

    def rim_wait(buf, send, recv, p):
        rim_wait_for(flat, send.at[p], recv.at[p])

    def back_copy(p, e, device):
        return pltpu.make_async_remote_copy(
            src_ref=U.at[p, W:W + T, W:W + T], dst_ref=G.at[p, pl.ds(T * e, T)],
            send_sem=g_send.at[p], recv_sem=g_recv.at[p, e], device_id=device, device_id_type=MESH)

    def back_start(p):
        @pl.when(other(giver))
        def _():
            back_copy(p, X % 2, giver).start()

        @pl.when(jnp.logical_not(other(giver)))
        def _():
            for x in range(T):
                G[p, T * (X % 2) + x] = U[p, W + x, W:W + T]

    def along_copy(p, e, source, YS):
        return pltpu.make_async_remote_copy(
            src_ref=G.at[p, T * e:T * e + T], dst_ref=out.at[T * e:T * e + T, pl.ds(T * (YS % 2), T)],
            send_sem=f_send.at[p, e], recv_sem=f_recv.at[source % 2, e], device_id=(p, gx, gy), device_id_type=MESH)

    def along_start(p, e):
        @pl.when(gives)
        def _():
            @pl.when(other(takers[e]))
            def _():
                back_copy(p, e, takers[e]).wait_recv()

            @pl.when(p != lvl)
            def _():
                along_copy(p, e, lvl, YA).start()

            @pl.when(p == lvl)
            def _():
                for x in range(T):
                    out[T * e + x, pl.ds(T * (YA % 2), T)] = G[p, T * e + x]

    lane = lax.broadcasted_iota(jnp.int32, (1, C, NZ), 2)
    first, last = lane == 0, lane == NZ - 1
    R = [(W, W + T) if x in (W - 1, W + T) else (W - 1, W + T + 1) for x in range(E)]

    def up(v):
        return pltpu.roll(v, 1, 2)

    def down(v):
        return pltpu.roll(v, NZ - 1, 2)

    def sweep(p, src, dst, rows, cols):
        for x in rows:
            lo, hi = cols(x)
            for a in range(lo, hi, 2):
                b = min(a + 2, hi)
                c = src(x, a - 1, b + 1)
                v, wz = c[1:-1], WZ[p, x, a:b]
                wy = WY[p, x, a - 1:b]
                n = (WX[p, x - 1, a:b] * src(x - 1, a, b) + WX[p, x, a:b] * src(x + 1, a, b)
                     + wy[:-1] * c[:-2] + wy[1:] * c[2:] + wz * up(v) + down(wz * v))
                dst(x, a, b, (RHS[p, x, a:b] + n) * INV[p, x, a:b])

    def split(u):
        hi = u.astype(jnp.bfloat16)
        lo = (u - hi.astype(jnp.float32)).astype(jnp.bfloat16)
        return jnp.concatenate([hi, lo, hi], axis=0)

    def chemistry(p):
        def one(get, put):
            u = get().reshape(4 * C, NZ)
            for k, w_ref, v in ((0, wf_ref, u), (1, wq_ref, u * u)):
                put(k, jnp.dot(w_ref[...], split(v), preferred_element_type=jnp.float32).reshape(4, C, NZ))

        for x in range(W - 1, W + T + 1):
            def put(k, v, x=x):
                PQ[k, x, W:W + T] = v
            one(lambda: U[p, x, W:W + T], put)
        for y in (W - 1, W + T):
            def put(k, v, y=y):
                for x in range(T):
                    PQ[k, W + x, y] = v[x]
            one(lambda: U[p, W:W + T, y], put)

    def setup(p):
        dh = dh_ref[...][None]
        lr = lr_ref[...][None]
        for x in range(E):
            lo, hi = (W, W + T) if x in (0, E - 1) else (R[x] if x in (1, E - 2) else (0, E))
            if x in (1, E - 2):
                lo, hi = 1, E - 1
            for a in range(lo, hi, 2):
                u = U[p, x, a:a + 2]
                K[x, a:a + 2] = dh + dh * (u * u)
        chemistry(p)
        for x in range(W - 1, W + T + 1):
            lo, hi = R[x]
            for a in range(lo, hi, 2):
                b = a + 2
                kc = K[x, a - 1:b + 1]
                k = kc[1:-1]
                kw, ke = K[x - 1, a:b], K[x + 1, a:b]
                ww, we, ws, wn = k + kw, k + ke, k + kc[:-2], k + kc[2:]
                kl = jnp.where(first, dh, up(k))
                kh = jnp.where(last, dh, down(k))
                wl = k + kl
                total = ((ww + we) + (ws + wn)) + (wl + (k + kh))
                wz = jnp.where(first, 0.0, wl)
                if x <= W + T - 1:
                    WX[p, x - 1, a:b] = ww
                if x >= W + T - 1:
                    WX[p, x, a:b] = we
                WY[p, x, a - 1:b - 1] = ws
                if b == hi:
                    WY[p, x, b - 1:b] = wn[-1:]
                WZ[p, x, a:b] = wz
                uc = U[p, x, a - 1:b + 1]
                u = uc[1:-1]
                n = (ww * U[p, x - 1, a:b] + we * U[p, x + 1, a:b] + ws * uc[:-2] + wn * uc[2:]
                     + wz * up(u) + down(wz * u))
                r = RF[x, a:b]
                made = r * PQ[0, x, a:b]
                lost = total + r * (lr + PQ[1, x, a:b])
                half = 0.5 * ((n + made) - lost * u)
                inv = 1.0 / (1.0 + lost)
                inflow = INF[x, a:b]
                old = ACC[p, x, a:b]
                right = (u + made) + inflow
                INF[x, a:b] = (old + half) - u
                ACC[p, x, a:b] = (half + u) + inflow
                RHS[p, x, a:b] = right
                INV[p, x, a:b] = inv
                V1[x, a:b] = (right + n) * inv

    none_v = jnp.zeros((1, C, NZ), jnp.float32)

    def mask(p):
        for cond, cells in ((X == 0, [(W - 1, y) for y in range(W, W + T)]),
                            (X == nx - 1, [(W + T, y) for y in range(W, W + T)]),
                            (Y == 0, [(x, W - 1) for x in range(W, W + T)]),
                            (Y == ny - 1, [(x, W + T) for x in range(W, W + T)])):
            @pl.when(cond)
            def _():
                for x, y in cells:
                    V1[x, y:y + 1] = none_v
                    INV[p, x, y:y + 1] = none_v

    inner = range(W, W + T)
    outer = range(W - 1, W + T + 1)

    def store_v1(x, a, b, v):
        V1[x, a:b] = v

    def phase_a(t, p):
        n = t - p

        @pl.when((n >= 0) & ((n < STEPS) | ((n == STEPS) & (p < LEVELS - 1))))
        def _():
            @pl.when(n == 0)
            def _():
                for x in range(E):
                    U[p, x] = S0[x, :, 0:C, :]

            @pl.when(n > 0)
            def _():
                rim_wait(U, u_send, u_recv, p)

            setup(p)

            @pl.when(n < STEPS)
            def _():
                mask(p)

                def put(x, a, b, v):
                    V2[p, x, a:b] = v
                sweep(p, lambda x, a, b: V1[x, a:b], put, inner, lambda x: (W, W + T))
                rim_start(V2, v_send, v_recv, p)

    def phase_b(t, p):
        n = t - p

        @pl.when((n >= 0) & (n < STEPS))
        def _():
            rim_wait(V2, v_send, v_recv, p)
            sweep(p, lambda x, a, b: V2[p, x, a:b], store_v1, outer, lambda x: R[x])

            def put(x, a, b, v):
                U[p, x, a:b] = v
            sweep(p, lambda x, a, b: V1[x, a:b], put, inner, lambda x: (W, W + T))

            @pl.when((n < STEPS - 1) | (p < LEVELS - 1))
            def _():
                rim_start(U, u_send, u_recv, p)

            @pl.when(n == STEPS - 1)
            def _():
                back_start(p)

    def tick(t, c):
        for x in range(1, E - 1):
            INF[x] = zero_v
        lax.fori_loop(0, LEVELS, lambda p, c: (phase_a(t, p), c)[1], 0)

        @pl.when(t >= LEVELS)
        def _():
            along_start(t - LEVELS, 0)

        lax.fori_loop(0, LEVELS, lambda p, c: (phase_b(t, p), c)[1], 0)

        @pl.when(t >= LEVELS)
        def _():
            along_start(t - LEVELS, 1)

        return c

    lax.fori_loop(0, STEPS + LEVELS - 1, tick, 0)

    for e in range(2):
        along_start(LEVELS - 1, e)

    first_source = 2 * ((gy + gy // 2) % 2)
    for k in range(2):
        source = first_source + k

        @pl.when(source != lvl)
        def _():
            for e in range(2):
                along_copy(lvl, e, source, source + (gy // 2) * (7 - 2 * source)).wait_recv()
    for p in range(LEVELS):
        @pl.when(other(giver))
        def _():
            back_copy(p, X % 2, giver).wait_send()

        @pl.when(gives & (p != lvl))
        def _():
            for e in range(2):
                along_copy(p, e, lvl, YA).wait_send()

    for e, device in enumerate(takers):
        @pl.when(gives & other(device))
        def _():
            hand(e, device).wait_send()


def on_device(nx, ny, initial, rate_factor, diffusivity, loss_rate, quench, formation):
    f32 = jnp.float32
    frame = (E, E, C, NZ)
    vmem = pl.BlockSpec(memory_space=pltpu.VMEM)
    dma = pltpu.SemaphoreType.DMA
    done = pl.pallas_call(
        functools.partial(kernel, nx, ny),
        name="deferred_correction",
        out_shape=jax.ShapeDtypeStruct((8, 8, C, NZ), f32),
        in_specs=[vmem] * 6,
        out_specs=vmem,
        scratch_shapes=[
            pltpu.VMEM((2, E, E, 24, NZ), f32),
            pltpu.VMEM((LEVELS,) + frame, f32),
            pltpu.VMEM((LEVELS,) + frame, f32),
            pltpu.VMEM(frame, f32),
            pltpu.VMEM(frame, f32),
            pltpu.VMEM((LEVELS,) + frame, f32),
            pltpu.VMEM((LEVELS,) + frame, f32),
            pltpu.VMEM((LEVELS,) + frame, f32),
            pltpu.VMEM((LEVELS,) + frame, f32),
            pltpu.VMEM((LEVELS,) + frame, f32),
            pltpu.VMEM((LEVELS,) + frame, f32),
            pltpu.VMEM(frame, f32),
            pltpu.VMEM((2,) + frame, f32),
            pltpu.VMEM(frame, f32),
            pltpu.VMEM((16 * W + 4, C, NZ), f32),
            pltpu.VMEM((16 * W + 4, 24, NZ), f32),
            pltpu.VMEM((C, NZ), f32), pltpu.VMEM((C, NZ), f32),
            pltpu.VMEM((4 * C, 12 * C), jnp.bfloat16), pltpu.VMEM((4 * C, 12 * C), jnp.bfloat16),
            pltpu.VMEM((LEVELS, 2 * T, T, C, NZ), f32),
            dma((3,)), dma((2,)),
            dma((LEVELS,)), dma((LEVELS,)),
            dma((LEVELS,)), dma((LEVELS,)),
            dma((LEVELS,)), dma((LEVELS, 2)),
            dma((LEVELS, 2)), dma((2, 2)),
        ],
        compiler_params=pltpu.CompilerParams(
            collective_id=0, has_side_effects=True, vmem_limit_bytes=44 << 20),
    )(initial, rate_factor, diffusivity[:, None], loss_rate[:, None], quench, formation)
    return done.transpose(2, 0, 1, 3)[None]


def solution(mesh):
    in_specs = (P(None, "gx", "gy", None), P("gx", "gy", None), P(), P(), P(), P())
    out_specs = P("lvl", None, "gx", "gy", None)
    nx, ny = 2 * mesh.shape["gx"], 2 * mesh.shape["gy"]
    return jax.shard_map(
        functools.partial(on_device, nx, ny), mesh=mesh, in_specs=in_specs, out_specs=out_specs, check_vma=False)
```

```python
import functools

import jax
import jax.numpy as jnp
from jax import lax
from jax.experimental import pallas as pl
from jax.experimental.pallas import tpu as pltpu
from jax.sharding import PartitionSpec as P

MESH = pl.DeviceIdType.MESH
REACT = 11
STEPS = 4
LEVELS = 4
C = 16
NZ = 128
T = 4
W = 2
E = T + 2 * W
DIRS = ((1, 1), (-1, -1), (1, -1), (-1, 1), (0, 1), (0, -1), (1, 0), (-1, 0))


def spans(d):
    if d == 1:
        return W + T - W, 0, W
    if d == -1:
        return W, W + T, W
    return W, W, T


def corner_spans(d):
    return (W + T - 1, W - 1, 1) if d == 1 else (W, W + T, 1)


def box(dx, dy):
    if dx and dy:
        return corner_spans(dx), corner_spans(dy)
    return spans(dx), spans(dy)


def here():
    lvl, gx, gy = lax.axis_index("lvl"), lax.axis_index("gx"), lax.axis_index("gy")
    y = gx % 4
    back = y // 2
    m = (y + back) % 2
    strip = 4 * (gx // 4) + m + (gy // 2) * (3 - 2 * m)
    return 2 * strip + gy % 2, lvl + back * (7 - 2 * lvl)


def device_at(X, Y):
    strip, back, r = X // 2, Y // 4, Y % 4
    s = strip % 4
    m = (s + s // 2) % 2
    y = m + back * (3 - 2 * m)
    return r + back * (3 - 2 * r), 4 * (strip // 4) + y, 2 * (s // 2) + X % 2


def kernel(nx, ny, ini, rf, d_ref, l_ref, quench_ref, formation_ref, out,
           stage, U, V2, V1, K, WX, WY, WZ, RHS, INV, ACC, INF, PQ, RF, flat, flat24,
           dh_ref, lr_ref, wq_ref, wf_ref, G,
           i_send, i_recv, u_send, u_recv, v_send, v_recv, g_send, g_recv, f_send, f_recv):
    lvl, gx, gy = lax.axis_index("lvl"), lax.axis_index("gx"), lax.axis_index("gy")
    me = (lvl, gx, gy)
    X, Y = here()

    def other(device):
        return (device[0] != lvl) | (device[1] != gx) | (device[2] != gy)

    def exists(dx, dy):
        ok = None
        for d, at, n in ((dx, X, nx), (dy, Y, ny)):
            if d:
                c = at < n - 1 if d == 1 else at > 0
                ok = c if ok is None else ok & c
        return ok

    beside = [(exists(dx, dy), device_at(X + dx, Y + dy)) for dx, dy in DIRS]
    gives = lvl // 2 == (gy + gy // 2) % 2
    YA = lvl + (gy // 2) * (7 - 2 * lvl)
    takers = [device_at(2 * gx + e, YA) for e in range(2)]
    giver = (lvl, X // 2, Y // 2)
    row_of_four = [((lvl + k) % LEVELS, gx, gy) for k in range(1, LEVELS)]

    def each(f):
        for i, (dx, dy) in enumerate(DIRS):
            @pl.when(beside[i][0])
            def _():
                f(i, dx, dy, beside[i][1])

    S0 = stage.at[1]
    zero = jnp.zeros((E, 24, NZ), jnp.float32)
    zero_v = jnp.zeros((E, C, NZ), jnp.float32)

    edge_x, edge_y = (X == 0) | (X == nx - 1), (Y == 0) | (Y == ny - 1)

    def clear(x, c):
        S0[x] = zero
        for p in range(LEVELS):
            V2[p, x] = zero_v
        return c

    @pl.when(edge_x | edge_y)
    def _():
        lax.fori_loop(0, E, clear, 0)

    bar = pltpu.get_barrier_semaphore()

    def greet(device):
        pl.semaphore_signal(bar, inc=1, device_id=device, device_id_type=MESH)

    each(lambda i, dx, dy, device: greet(device))
    others = [(lvl >= 0, device) for device in row_of_four]
    others += [(gives & other(device), device) for device in takers] + [(other(giver), giver)]
    for cond, device in others:
        @pl.when(cond)
        def _():
            greet(device)

    reacts = lax.broadcasted_iota(jnp.int32, (C, NZ), 0) < REACT
    dh_ref[...] = jnp.broadcast_to(0.5 * d_ref[...], (C, NZ))
    lr_ref[...] = jnp.where(reacts, jnp.broadcast_to(l_ref[...], (C, NZ)), 0.0)
    row, col = (lax.broadcasted_iota(jnp.int32, (4 * C, 4 * C), k) for k in range(2))
    for w_ref, m in ((wq_ref, quench_ref[...] * l_ref[...]), (wf_ref, formation_ref[...])):
        m = jnp.concatenate([jnp.concatenate([m] * 4, axis=1)] * 4, axis=0)
        m = jnp.where((row // C == col // C) & (row % C < REACT), m, 0.0)
        hi = m.astype(jnp.bfloat16).astype(jnp.float32)
        w_ref[...] = jnp.concatenate([hi, hi, m - hi], axis=1).astype(jnp.bfloat16)

    nat = stage.at[0]
    for x in range(8):
        nat[x, :, 0:C, :] = jnp.swapaxes(ini[:, x], 0, 1)
        nat[x, :, C:24, :] = jnp.broadcast_to(rf[x][:, None, :], (8, 8, NZ))

    count = sum(ok.astype(jnp.int32) for ok, _ in beside) + sum(cond.astype(jnp.int32) for cond, _ in others)
    pl.semaphore_wait(bar, count)

    def hand(e, device):
        return pltpu.make_async_remote_copy(
            src_ref=nat.at[T * e:T * e + T, pl.ds(T * (YA % 2), T)],
            dst_ref=S0.at[W:W + T, W:W + T],
            send_sem=i_send.at[1 + e], recv_sem=i_recv.at[1], device_id=device, device_id_type=MESH)

    for e, device in enumerate(takers):
        @pl.when(gives & other(device))
        def _():
            hand(e, device).start()

        @pl.when(gives & jnp.logical_not(other(device)))
        def _():
            for x in range(T):
                S0[W + x, W:W + T] = nat[T * e + x, pl.ds(T * (YA % 2), T)]

    @pl.when(other(giver))
    def _():
        hand(0, giver).wait_recv()

    def rim_copy(ref, send, recv, dx, dy, device):
        (sx, tx, mx), (sy, ty, my) = box(dx, dy)
        return pltpu.make_async_remote_copy(
            src_ref=ref.at[sx:sx + mx, sy:sy + my], dst_ref=ref.at[tx:tx + mx, ty:ty + my],
            send_sem=send, recv_sem=recv, device_id=device, device_id_type=MESH)

    inside = jnp.logical_not(edge_x | edge_y)
    at_corner = edge_x & edge_y
    at_edge = (edge_x | edge_y) & jnp.logical_not(at_corner)

    def rim_wait_for(ref, send, recv):
        for cond, cells in ((inside, 8 * W + 8 * W + 4), (at_edge, 12 * W + 2), (at_corner, 8 * W + 1)):
            @pl.when(cond)
            def _():
                copy = pltpu.make_async_remote_copy(
                    src_ref=ref.at[0:cells], dst_ref=ref.at[0:cells],
                    send_sem=send, recv_sem=recv, device_id=me, device_id_type=MESH)
                copy.wait_recv()
                copy.wait_send()

    each(lambda i, dx, dy, device: rim_copy(S0, i_send.at[0], i_recv.at[0], dx, dy, device).start())
    rim_wait_for(flat24, i_send.at[0], i_recv.at[0])
    for x in range(E):
        for h in range(2):
            RF[x, :, 8 * h:8 * h + 8, :] = S0[x, :, C:24, :]

    def rim_start(buf, send, recv, p):
        each(lambda i, dx, dy, device: rim_copy(buf.at[p], send.at[p], recv.at[p], dx, dy, device).start())

    def rim_wait(buf, send, recv, p):
        rim_wait_for(flat, send.at[p], recv.at[p])

    def back_copy(p, e, device):
        return pltpu.make_async_remote_copy(
            src_ref=U.at[p, W:W + T, W:W + T], dst_ref=G.at[p, pl.ds(T * e, T)],
            send_sem=g_send.at[p], recv_sem=g_recv.at[p, e], device_id=device, device_id_type=MESH)

    def back_start(p):
        @pl.when(other(giver))
        def _():
            back_copy(p, X % 2, giver).start()

        @pl.when(jnp.logical_not(other(giver)))
        def _():
            for x in range(T):
                G[p, T * (X % 2) + x] = U[p, W + x, W:W + T]

    def along_copy(p, e, source, YS):
        return pltpu.make_async_remote_copy(
            src_ref=G.at[p, T * e:T * e + T], dst_ref=out.at[T * e:T * e + T, pl.ds(T * (YS % 2), T)],
            send_sem=f_send.at[p, e], recv_sem=f_recv.at[source % 2, e], device_id=(p, gx, gy), device_id_type=MESH)

    def along_start(p, e):
        @pl.when(gives)
        def _():
            @pl.when(other(takers[e]))
            def _():
                back_copy(p, e, takers[e]).wait_recv()

            @pl.when(p != lvl)
            def _():
                along_copy(p, e, lvl, YA).start()

            @pl.when(p == lvl)
            def _():
                for x in range(T):
                    out[T * e + x, pl.ds(T * (YA % 2), T)] = G[p, T * e + x]

    lane = lax.broadcasted_iota(jnp.int32, (1, C, NZ), 2)
    first, last = lane == 0, lane == NZ - 1
    R = [(W, W + T) if x in (W - 1, W + T) else (W - 1, W + T + 1) for x in range(E)]

    def up(v):
        return pltpu.roll(v, 1, 2)

    def down(v):
        return pltpu.roll(v, NZ - 1, 2)

    def sweep(p, src, dst, rows, cols):
        for x in rows:
            lo, hi = cols(x)
            for a in range(lo, hi, 2):
                b = min(a + 2, hi)
                c = src(x, a - 1, b + 1)
                v, wz = c[1:-1], WZ[p, x, a:b]
                wy = WY[p, x, a - 1:b]
                n = (WX[p, x - 1, a:b] * src(x - 1, a, b) + WX[p, x, a:b] * src(x + 1, a, b)
                     + wy[:-1] * c[:-2] + wy[1:] * c[2:] + wz * up(v) + down(wz * v))
                dst(x, a, b, (RHS[p, x, a:b] + n) * INV[p, x, a:b])

    def split(u):
        hi = u.astype(jnp.bfloat16)
        lo = (u - hi.astype(jnp.float32)).astype(jnp.bfloat16)
        return jnp.concatenate([hi, lo, hi], axis=0)

    def chemistry(p):
        def one(get, put):
            u = get().reshape(4 * C, NZ)
            for k, w_ref, v in ((0, wf_ref, u), (1, wq_ref, u * u)):
                put(k, jnp.dot(w_ref[...], split(v), preferred_element_type=jnp.float32).reshape(4, C, NZ))

        for x in range(W - 1, W + T + 1):
            def put(k, v, x=x):
                PQ[k, x, W:W + T] = v
            one(lambda: U[p, x, W:W + T], put)
        for y in (W - 1, W + T):
            def put(k, v, y=y):
                for x in range(T):
                    PQ[k, W + x, y] = v[x]
            one(lambda: U[p, W:W + T, y], put)

    def setup(p):
        dh = dh_ref[...][None]
        lr = lr_ref[...][None]
        for x in range(E):
            lo, hi = (W, W + T) if x in (0, E - 1) else (R[x] if x in (1, E - 2) else (0, E))
            if x in (1, E - 2):
                lo, hi = 1, E - 1
            for a in range(lo, hi, 2):
                u = U[p, x, a:a + 2]
                K[x, a:a + 2] = dh + dh * (u * u)
        chemistry(p)
        for x in range(W - 1, W + T + 1):
            lo, hi = R[x]
            for a in range(lo, hi, 2):
                b = a + 2
                kc = K[x, a - 1:b + 1]
                k = kc[1:-1]
                kw, ke = K[x - 1, a:b], K[x + 1, a:b]
                ww, we, ws, wn = k + kw, k + ke, k + kc[:-2], k + kc[2:]
                kl = jnp.where(first, dh, up(k))
                kh = jnp.where(last, dh, down(k))
                wl = k + kl
                total = ((ww + we) + (ws + wn)) + (wl + (k + kh))
                wz = jnp.where(first, 0.0, wl)
                if x <= W + T - 1:
                    WX[p, x - 1, a:b] = ww
                if x >= W + T - 1:
                    WX[p, x, a:b] = we
                WY[p, x, a - 1:b - 1] = ws
                if b == hi:
                    WY[p, x, b - 1:b] = wn[-1:]
                WZ[p, x, a:b] = wz
                uc = U[p, x, a - 1:b + 1]
                u = uc[1:-1]
                n = (ww * U[p, x - 1, a:b] + we * U[p, x + 1, a:b] + ws * uc[:-2] + wn * uc[2:]
                     + wz * up(u) + down(wz * u))
                r = RF[x, a:b]
                made = r * PQ[0, x, a:b]
                lost = total + r * (lr + PQ[1, x, a:b])
                half = 0.5 * ((n + made) - lost * u)
                inv = 1.0 / (1.0 + lost)
                inflow = INF[x, a:b]
                old = ACC[p, x, a:b]
                right = (u + made) + inflow
                INF[x, a:b] = (old + half) - u
                ACC[p, x, a:b] = (half + u) + inflow
                RHS[p, x, a:b] = right
                INV[p, x, a:b] = inv
                V1[x, a:b] = (right + n) * inv

    none_v = jnp.zeros((1, C, NZ), jnp.float32)

    def mask(p):
        for cond, cells in ((X == 0, [(W - 1, y) for y in range(W, W + T)]),
                            (X == nx - 1, [(W + T, y) for y in range(W, W + T)]),
                            (Y == 0, [(x, W - 1) for x in range(W, W + T)]),
                            (Y == ny - 1, [(x, W + T) for x in range(W, W + T)])):
            @pl.when(cond)
            def _():
                for x, y in cells:
                    V1[x, y:y + 1] = none_v
                    INV[p, x, y:y + 1] = none_v

    inner = range(W, W + T)
    outer = range(W - 1, W + T + 1)

    def store_v1(x, a, b, v):
        V1[x, a:b] = v

    def phase_a(t, p):
        n = t - p

        @pl.when((n >= 0) & ((n < STEPS) | ((n == STEPS) & (p < LEVELS - 1))))
        def _():
            @pl.when(n == 0)
            def _():
                for x in range(E):
                    U[p, x] = S0[x, :, 0:C, :]

            @pl.when(n > 0)
            def _():
                rim_wait(U, u_send, u_recv, p)

            setup(p)

            @pl.when(n < STEPS)
            def _():
                mask(p)

                def put(x, a, b, v):
                    V2[p, x, a:b] = v
                sweep(p, lambda x, a, b: V1[x, a:b], put, inner, lambda x: (W, W + T))
                rim_start(V2, v_send, v_recv, p)

    def phase_b(t, p):
        n = t - p

        @pl.when((n >= 0) & (n < STEPS))
        def _():
            rim_wait(V2, v_send, v_recv, p)
            sweep(p, lambda x, a, b: V2[p, x, a:b], store_v1, outer, lambda x: R[x])

            def put(x, a, b, v):
                U[p, x, a:b] = v
            sweep(p, lambda x, a, b: V1[x, a:b], put, inner, lambda x: (W, W + T))

            @pl.when((n < STEPS - 1) | (p < LEVELS - 1))
            def _():
                rim_start(U, u_send, u_recv, p)

            @pl.when(n == STEPS - 1)
            def _():
                back_start(p)

    def tick(t, c):
        for x in range(1, E - 1):
            INF[x] = zero_v
        lax.fori_loop(0, LEVELS, lambda p, c: (phase_a(t, p), c)[1], 0)

        @pl.when(t >= LEVELS)
        def _():
            along_start(t - LEVELS, 0)

        lax.fori_loop(0, LEVELS, lambda p, c: (phase_b(t, p), c)[1], 0)

        @pl.when(t >= LEVELS)
        def _():
            along_start(t - LEVELS, 1)

        return c

    lax.fori_loop(0, STEPS + LEVELS - 1, tick, 0)

    for e in range(2):
        along_start(LEVELS - 1, e)

    first_source = 2 * ((gy + gy // 2) % 2)
    for k in range(2):
        source = first_source + k

        @pl.when(source != lvl)
        def _():
            for e in range(2):
                along_copy(lvl, e, source, source + (gy // 2) * (7 - 2 * source)).wait_recv()
    for p in range(LEVELS):
        @pl.when(other(giver))
        def _():
            back_copy(p, X % 2, giver).wait_send()

        @pl.when(gives & (p != lvl))
        def _():
            for e in range(2):
                along_copy(p, e, lvl, YA).wait_send()

    for e, device in enumerate(takers):
        @pl.when(gives & other(device))
        def _():
            hand(e, device).wait_send()


def on_device(nx, ny, initial, rate_factor, diffusivity, loss_rate, quench, formation):
    f32 = jnp.float32
    frame = (E, E, C, NZ)
    vmem = pl.BlockSpec(memory_space=pltpu.VMEM)
    dma = pltpu.SemaphoreType.DMA
    done = pl.pallas_call(
        functools.partial(kernel, nx, ny),
        name="deferred_correction",
        out_shape=jax.ShapeDtypeStruct((8, 8, C, NZ), f32),
        in_specs=[vmem] * 6,
        out_specs=vmem,
        scratch_shapes=[
            pltpu.VMEM((2, E, E, 24, NZ), f32),
            pltpu.VMEM((LEVELS,) + frame, f32),
            pltpu.VMEM((LEVELS,) + frame, f32),
            pltpu.VMEM(frame, f32),
            pltpu.VMEM(frame, f32),
            pltpu.VMEM((LEVELS,) + frame, f32),
            pltpu.VMEM((LEVELS,) + frame, f32),
            pltpu.VMEM((LEVELS,) + frame, f32),
            pltpu.VMEM((LEVELS,) + frame, f32),
            pltpu.VMEM((LEVELS,) + frame, f32),
            pltpu.VMEM((LEVELS,) + frame, f32),
            pltpu.VMEM(frame, f32),
            pltpu.VMEM((2,) + frame, f32),
            pltpu.VMEM(frame, f32),
            pltpu.VMEM((16 * W + 4, C, NZ), f32),
            pltpu.VMEM((16 * W + 4, 24, NZ), f32),
            pltpu.VMEM((C, NZ), f32), pltpu.VMEM((C, NZ), f32),
            pltpu.VMEM((4 * C, 12 * C), jnp.bfloat16), pltpu.VMEM((4 * C, 12 * C), jnp.bfloat16),
            pltpu.VMEM((LEVELS, 2 * T, T, C, NZ), f32),
            dma((3,)), dma((2,)),
            dma((LEVELS,)), dma((LEVELS,)),
            dma((LEVELS,)), dma((LEVELS,)),
            dma((LEVELS,)), dma((LEVELS, 2)),
            dma((LEVELS, 2)), dma((2, 2)),
        ],
        compiler_params=pltpu.CompilerParams(
            collective_id=0, has_side_effects=True, vmem_limit_bytes=44 << 20),
    )(initial, rate_factor, diffusivity[:, None], loss_rate[:, None], quench, formation)
    return done.transpose(2, 0, 1, 3)[None]


def solution(mesh):
    in_specs = (P(None, "gx", "gy", None), P("gx", "gy", None), P(), P(), P(), P())
    out_specs = P("lvl", None, "gx", "gy", None)
    nx, ny = 2 * mesh.shape["gx"], 2 * mesh.shape["gy"]
    return jax.shard_map(
        functools.partial(on_device, nx, ny), mesh=mesh, in_specs=in_specs, out_specs=out_specs, check_vma=False)
```

```python
import functools

import jax
import jax.numpy as jnp
from jax import lax
from jax.experimental import pallas as pl
from jax.experimental.pallas import tpu as pltpu
from jax.sharding import PartitionSpec as P

MESH = pl.DeviceIdType.MESH
REACT = 11
STEPS = 4
LEVELS = 4
C = 16
NZ = 128
T = 4
W = 2
E = T + 2 * W
DIRS = ((1, 1), (-1, -1), (1, -1), (-1, 1), (0, 1), (0, -1), (1, 0), (-1, 0))


def spans(d):
    if d == 1:
        return W + T - W, 0, W
    if d == -1:
        return W, W + T, W
    return W, W, T


def corner_spans(d):
    return (W + T - 1, W - 1, 1) if d == 1 else (W, W + T, 1)


def box(dx, dy):
    if dx and dy:
        return corner_spans(dx), corner_spans(dy)
    return spans(dx), spans(dy)


def here():
    lvl, gx, gy = lax.axis_index("lvl"), lax.axis_index("gx"), lax.axis_index("gy")
    y = gx % 4
    back = y // 2
    m = (y + back) % 2
    strip = 4 * (gx // 4) + m + (gy // 2) * (3 - 2 * m)
    return 2 * strip + gy % 2, lvl + back * (7 - 2 * lvl)


def device_at(X, Y):
    strip, back, r = X // 2, Y // 4, Y % 4
    s = strip % 4
    m = (s + s // 2) % 2
    y = m + back * (3 - 2 * m)
    return r + back * (3 - 2 * r), 4 * (strip // 4) + y, 2 * (s // 2) + X % 2


def kernel(nx, ny, ini, rf, d_ref, l_ref, quench_ref, formation_ref, out,
           stage, U, V2, V1, K, WX, WY, WZ, RHS, INV, ACC, INF, PQ, RF, flat, flat24,
           dh_ref, lr_ref, wq_ref, wf_ref, G,
           i_send, i_recv, u_send, u_recv, v_send, v_recv, g_send, g_recv, f_send, f_recv):
    lvl, gx, gy = lax.axis_index("lvl"), lax.axis_index("gx"), lax.axis_index("gy")
    me = (lvl, gx, gy)
    X, Y = here()

    def other(device):
        return (device[0] != lvl) | (device[1] != gx) | (device[2] != gy)

    def exists(dx, dy):
        ok = None
        for d, at, n in ((dx, X, nx), (dy, Y, ny)):
            if d:
                c = at < n - 1 if d == 1 else at > 0
                ok = c if ok is None else ok & c
        return ok

    beside = [(exists(dx, dy), device_at(X + dx, Y + dy)) for dx, dy in DIRS]
    gives = lvl // 2 == (gy + gy // 2) % 2
    YA = lvl + (gy // 2) * (7 - 2 * lvl)
    takers = [device_at(2 * gx + e, YA) for e in range(2)]
    giver = (lvl, X // 2, Y // 2)
    row_of_four = [((lvl + k) % LEVELS, gx, gy) for k in range(1, LEVELS)]

    def each(f):
        for i, (dx, dy) in enumerate(DIRS):
            @pl.when(beside[i][0])
            def _():
                f(i, dx, dy, beside[i][1])

    S0 = stage.at[1]
    zero = jnp.zeros((E, 24, NZ), jnp.float32)
    zero_v = jnp.zeros((E, C, NZ), jnp.float32)

    edge_x, edge_y = (X == 0) | (X == nx - 1), (Y == 0) | (Y == ny - 1)

    def clear(x, c):
        S0[x] = zero
        for p in range(LEVELS):
            V2[p, x] = zero_v
        return c

    @pl.when(edge_x | edge_y)
    def _():
        lax.fori_loop(0, E, clear, 0)

    bar = pltpu.get_barrier_semaphore()

    def greet(device):
        pl.semaphore_signal(bar, inc=1, device_id=device, device_id_type=MESH)

    each(lambda i, dx, dy, device: greet(device))
    others = [(lvl >= 0, device) for device in row_of_four]
    others += [(gives & other(device), device) for device in takers] + [(other(giver), giver)]
    for cond, device in others:
        @pl.when(cond)
        def _():
            greet(device)

    reacts = lax.broadcasted_iota(jnp.int32, (C, NZ), 0) < REACT
    dh_ref[...] = jnp.broadcast_to(0.5 * d_ref[...], (C, NZ))
    lr_ref[...] = jnp.where(reacts, jnp.broadcast_to(l_ref[...], (C, NZ)), 0.0)
    row, col = (lax.broadcasted_iota(jnp.int32, (4 * C, 4 * C), k) for k in range(2))
    for w_ref, m in ((wq_ref, quench_ref[...] * l_ref[...]), (wf_ref, formation_ref[...])):
        m = jnp.concatenate([jnp.concatenate([m] * 4, axis=1)] * 4, axis=0)
        m = jnp.where((row // C == col // C) & (row % C < REACT), m, 0.0)
        hi = m.astype(jnp.bfloat16).astype(jnp.float32)
        w_ref[...] = jnp.concatenate([hi, hi, m - hi], axis=1).astype(jnp.bfloat16)

    nat = stage.at[0]
    for x in range(8):
        nat[x, :, 0:C, :] = jnp.swapaxes(ini[:, x], 0, 1)
        nat[x, :, C:24, :] = jnp.broadcast_to(rf[x][:, None, :], (8, 8, NZ))

    count = sum(ok.astype(jnp.int32) for ok, _ in beside) + sum(cond.astype(jnp.int32) for cond, _ in others)
    pl.semaphore_wait(bar, count)

    def hand(e, device):
        return pltpu.make_async_remote_copy(
            src_ref=nat.at[T * e:T * e + T, pl.ds(T * (YA % 2), T)],
            dst_ref=S0.at[W:W + T, W:W + T],
            send_sem=i_send.at[1 + e], recv_sem=i_recv.at[1], device_id=device, device_id_type=MESH)

    for e, device in enumerate(takers):
        @pl.when(gives & other(device))
        def _():
            hand(e, device).start()

        @pl.when(gives & jnp.logical_not(other(device)))
        def _():
            for x in range(T):
                S0[W + x, W:W + T] = nat[T * e + x, pl.ds(T * (YA % 2), T)]

    @pl.when(other(giver))
    def _():
        hand(0, giver).wait_recv()

    def rim_copy(ref, send, recv, dx, dy, device):
        (sx, tx, mx), (sy, ty, my) = box(dx, dy)
        return pltpu.make_async_remote_copy(
            src_ref=ref.at[sx:sx + mx, sy:sy + my], dst_ref=ref.at[tx:tx + mx, ty:ty + my],
            send_sem=send, recv_sem=recv, device_id=device, device_id_type=MESH)

    inside = jnp.logical_not(edge_x | edge_y)
    at_corner = edge_x & edge_y
    at_edge = (edge_x | edge_y) & jnp.logical_not(at_corner)

    def rim_wait_for(ref, send, recv):
        for cond, cells in ((inside, 8 * W + 8 * W + 4), (at_edge, 12 * W + 2), (at_corner, 8 * W + 1)):
            @pl.when(cond)
            def _():
                copy = pltpu.make_async_remote_copy(
                    src_ref=ref.at[0:cells], dst_ref=ref.at[0:cells],
                    send_sem=send, recv_sem=recv, device_id=me, device_id_type=MESH)
                copy.wait_recv()
                copy.wait_send()

    each(lambda i, dx, dy, device: rim_copy(S0, i_send.at[0], i_recv.at[0], dx, dy, device).start())
    rim_wait_for(flat24, i_send.at[0], i_recv.at[0])
    for x in range(E):
        for h in range(2):
            RF[x, :, 8 * h:8 * h + 8, :] = S0[x, :, C:24, :]

    def rim_start(buf, send, recv, p):
        each(lambda i, dx, dy, device: rim_copy(buf.at[p], send.at[p], recv.at[p], dx, dy, device).start())

    def rim_wait(buf, send, recv, p):
        rim_wait_for(flat, send.at[p], recv.at[p])

    def back_copy(p, e, device):
        return pltpu.make_async_remote_copy(
            src_ref=U.at[p, W:W + T, W:W + T], dst_ref=G.at[p, pl.ds(T * e, T)],
            send_sem=g_send.at[p], recv_sem=g_recv.at[p, e], device_id=device, device_id_type=MESH)

    def back_start(p):
        @pl.when(other(giver))
        def _():
            back_copy(p, X % 2, giver).start()

        @pl.when(jnp.logical_not(other(giver)))
        def _():
            for x in range(T):
                G[p, T * (X % 2) + x] = U[p, W + x, W:W + T]

    def along_copy(p, e, source, YS):
        return pltpu.make_async_remote_copy(
            src_ref=G.at[p, T * e:T * e + T], dst_ref=out.at[T * e:T * e + T, pl.ds(T * (YS % 2), T)],
            send_sem=f_send.at[p, e], recv_sem=f_recv.at[source % 2, e], device_id=(p, gx, gy), device_id_type=MESH)

    def along_start(p, e):
        @pl.when(gives)
        def _():
            @pl.when(other(takers[e]))
            def _():
                back_copy(p, e, takers[e]).wait_recv()

            @pl.when(p != lvl)
            def _():
                along_copy(p, e, lvl, YA).start()

            @pl.when(p == lvl)
            def _():
                for x in range(T):
                    out[T * e + x, pl.ds(T * (YA % 2), T)] = G[p, T * e + x]

    lane = lax.broadcasted_iota(jnp.int32, (1, C, NZ), 2)
    first, last = lane == 0, lane == NZ - 1
    R = [(W, W + T) if x in (W - 1, W + T) else (W - 1, W + T + 1) for x in range(E)]

    def up(v):
        return pltpu.roll(v, 1, 2)

    def down(v):
        return pltpu.roll(v, NZ - 1, 2)

    def sweep(p, src, dst, rows, cols):
        for x in rows:
            lo, hi = cols(x)
            for a in range(lo, hi, 2):
                b = min(a + 2, hi)
                c = src(x, a - 1, b + 1)
                v, wz = c[1:-1], WZ[p, x, a:b]
                wy = WY[p, x, a - 1:b]
                n = (WX[p, x - 1, a:b] * src(x - 1, a, b) + WX[p, x, a:b] * src(x + 1, a, b)
                     + wy[:-1] * c[:-2] + wy[1:] * c[2:] + wz * up(v) + down(wz * v))
                dst(x, a, b, (RHS[p, x, a:b] + n) * INV[p, x, a:b])

    def split(u):
        hi = u.astype(jnp.bfloat16)
        lo = (u - hi.astype(jnp.float32)).astype(jnp.bfloat16)
        return jnp.concatenate([hi, lo, hi], axis=0)

    def chemistry(p):
        def one(get, put):
            u = get().reshape(4 * C, NZ)
            for k, w_ref, v in ((0, wf_ref, u), (1, wq_ref, u * u)):
                put(k, jnp.dot(w_ref[...], split(v), preferred_element_type=jnp.float32).reshape(4, C, NZ))

        for x in range(W - 1, W + T + 1):
            def put(k, v, x=x):
                PQ[k, x, W:W + T] = v
            one(lambda: U[p, x, W:W + T], put)
        for y in (W - 1, W + T):
            def put(k, v, y=y):
                for x in range(T):
                    PQ[k, W + x, y] = v[x]
            one(lambda: U[p, W:W + T, y], put)

    def setup(p):
        dh = dh_ref[...][None]
        lr = lr_ref[...][None]
        for x in range(E):
            lo, hi = (W, W + T) if x in (0, E - 1) else (R[x] if x in (1, E - 2) else (0, E))
            if x in (1, E - 2):
                lo, hi = 1, E - 1
            for a in range(lo, hi, 2):
                u = U[p, x, a:a + 2]
                K[x, a:a + 2] = dh + dh * (u * u)
        chemistry(p)
        for x in range(W - 1, W + T + 1):
            lo, hi = R[x]
            for a in range(lo, hi, hi - lo):
                b = hi
                kc = K[x, a - 1:b + 1]
                k = kc[1:-1]
                kw, ke = K[x - 1, a:b], K[x + 1, a:b]
                ww, we, ws, wn = k + kw, k + ke, k + kc[:-2], k + kc[2:]
                kl = jnp.where(first, dh, up(k))
                kh = jnp.where(last, dh, down(k))
                wl = k + kl
                total = ((ww + we) + (ws + wn)) + (wl + (k + kh))
                wz = jnp.where(first, 0.0, wl)
                if x <= W + T - 1:
                    WX[p, x - 1, a:b] = ww
                if x >= W + T - 1:
                    WX[p, x, a:b] = we
                WY[p, x, a - 1:b - 1] = ws
                if b == hi:
                    WY[p, x, b - 1:b] = wn[-1:]
                WZ[p, x, a:b] = wz
                uc = U[p, x, a - 1:b + 1]
                u = uc[1:-1]
                n = (ww * U[p, x - 1, a:b] + we * U[p, x + 1, a:b] + ws * uc[:-2] + wn * uc[2:]
                     + wz * up(u) + down(wz * u))
                r = RF[x, a:b]
                made = r * PQ[0, x, a:b]
                lost = total + r * (lr + PQ[1, x, a:b])
                half = 0.5 * ((n + made) - lost * u)
                inv = 1.0 / (1.0 + lost)
                inflow = INF[x, a:b]
                old = ACC[p, x, a:b]
                right = (u + made) + inflow
                INF[x, a:b] = (old + half) - u
                ACC[p, x, a:b] = (half + u) + inflow
                RHS[p, x, a:b] = right
                INV[p, x, a:b] = inv
                V1[x, a:b] = (right + n) * inv

    none_v = jnp.zeros((1, C, NZ), jnp.float32)

    def mask(p):
        for cond, cells in ((X == 0, [(W - 1, y) for y in range(W, W + T)]),
                            (X == nx - 1, [(W + T, y) for y in range(W, W + T)]),
                            (Y == 0, [(x, W - 1) for x in range(W, W + T)]),
                            (Y == ny - 1, [(x, W + T) for x in range(W, W + T)])):
            @pl.when(cond)
            def _():
                for x, y in cells:
                    V1[x, y:y + 1] = none_v
                    INV[p, x, y:y + 1] = none_v

    inner = range(W, W + T)
    outer = range(W - 1, W + T + 1)

    def store_v1(x, a, b, v):
        V1[x, a:b] = v

    def phase_a(t, p):
        n = t - p

        @pl.when((n >= 0) & ((n < STEPS) | ((n == STEPS) & (p < LEVELS - 1))))
        def _():
            @pl.when(n == 0)
            def _():
                for x in range(E):
                    U[p, x] = S0[x, :, 0:C, :]

            @pl.when(n > 0)
            def _():
                rim_wait(U, u_send, u_recv, p)

            setup(p)

            @pl.when(n < STEPS)
            def _():
                mask(p)

                def put(x, a, b, v):
                    V2[p, x, a:b] = v
                sweep(p, lambda x, a, b: V1[x, a:b], put, inner, lambda x: (W, W + T))
                rim_start(V2, v_send, v_recv, p)

    def phase_b(t, p):
        n = t - p

        @pl.when((n >= 0) & (n < STEPS))
        def _():
            rim_wait(V2, v_send, v_recv, p)
            sweep(p, lambda x, a, b: V2[p, x, a:b], store_v1, outer, lambda x: R[x])

            def put(x, a, b, v):
                U[p, x, a:b] = v
            sweep(p, lambda x, a, b: V1[x, a:b], put, inner, lambda x: (W, W + T))

            @pl.when((n < STEPS - 1) | (p < LEVELS - 1))
            def _():
                rim_start(U, u_send, u_recv, p)

            @pl.when(n == STEPS - 1)
            def _():
                back_start(p)

    def tick(t, c):
        for x in range(1, E - 1):
            INF[x] = zero_v
        lax.fori_loop(0, LEVELS, lambda p, c: (phase_a(t, p), c)[1], 0)

        @pl.when(t >= LEVELS)
        def _():
            along_start(t - LEVELS, 0)

        lax.fori_loop(0, LEVELS, lambda p, c: (phase_b(t, p), c)[1], 0)

        @pl.when(t >= LEVELS)
        def _():
            along_start(t - LEVELS, 1)

        return c

    lax.fori_loop(0, STEPS + LEVELS - 1, tick, 0)

    for e in range(2):
        along_start(LEVELS - 1, e)

    first_source = 2 * ((gy + gy // 2) % 2)
    for k in range(2):
        source = first_source + k

        @pl.when(source != lvl)
        def _():
            for e in range(2):
                along_copy(lvl, e, source, source + (gy // 2) * (7 - 2 * source)).wait_recv()
    for p in range(LEVELS):
        @pl.when(other(giver))
        def _():
            back_copy(p, X % 2, giver).wait_send()

        @pl.when(gives & (p != lvl))
        def _():
            for e in range(2):
                along_copy(p, e, lvl, YA).wait_send()

    for e, device in enumerate(takers):
        @pl.when(gives & other(device))
        def _():
            hand(e, device).wait_send()


def on_device(nx, ny, initial, rate_factor, diffusivity, loss_rate, quench, formation):
    f32 = jnp.float32
    frame = (E, E, C, NZ)
    vmem = pl.BlockSpec(memory_space=pltpu.VMEM)
    dma = pltpu.SemaphoreType.DMA
    done = pl.pallas_call(
        functools.partial(kernel, nx, ny),
        name="deferred_correction",
        out_shape=jax.ShapeDtypeStruct((8, 8, C, NZ), f32),
        in_specs=[vmem] * 6,
        out_specs=vmem,
        scratch_shapes=[
            pltpu.VMEM((2, E, E, 24, NZ), f32),
            pltpu.VMEM((LEVELS,) + frame, f32),
            pltpu.VMEM((LEVELS,) + frame, f32),
            pltpu.VMEM(frame, f32),
            pltpu.VMEM(frame, f32),
            pltpu.VMEM((LEVELS,) + frame, f32),
            pltpu.VMEM((LEVELS,) + frame, f32),
            pltpu.VMEM((LEVELS,) + frame, f32),
            pltpu.VMEM((LEVELS,) + frame, f32),
            pltpu.VMEM((LEVELS,) + frame, f32),
            pltpu.VMEM((LEVELS,) + frame, f32),
            pltpu.VMEM(frame, f32),
            pltpu.VMEM((2,) + frame, f32),
            pltpu.VMEM(frame, f32),
            pltpu.VMEM((16 * W + 4, C, NZ), f32),
            pltpu.VMEM((16 * W + 4, 24, NZ), f32),
            pltpu.VMEM((C, NZ), f32), pltpu.VMEM((C, NZ), f32),
            pltpu.VMEM((4 * C, 12 * C), jnp.bfloat16), pltpu.VMEM((4 * C, 12 * C), jnp.bfloat16),
            pltpu.VMEM((LEVELS, 2 * T, T, C, NZ), f32),
            dma((3,)), dma((2,)),
            dma((LEVELS,)), dma((LEVELS,)),
            dma((LEVELS,)), dma((LEVELS,)),
            dma((LEVELS,)), dma((LEVELS, 2)),
            dma((LEVELS, 2)), dma((2, 2)),
        ],
        compiler_params=pltpu.CompilerParams(
            collective_id=0, has_side_effects=True, vmem_limit_bytes=44 << 20),
    )(initial, rate_factor, diffusivity[:, None], loss_rate[:, None], quench, formation)
    return done.transpose(2, 0, 1, 3)[None]


def solution(mesh):
    in_specs = (P(None, "gx", "gy", None), P("gx", "gy", None), P(), P(), P(), P())
    out_specs = P("lvl", None, "gx", "gy", None)
    nx, ny = 2 * mesh.shape["gx"], 2 * mesh.shape["gy"]
    return jax.shard_map(
        functools.partial(on_device, nx, ny), mesh=mesh, in_specs=in_specs, out_specs=out_specs, check_vma=False)
```

```python
import functools

import jax
import jax.numpy as jnp
from jax import lax
from jax.experimental import pallas as pl
from jax.experimental.pallas import tpu as pltpu
from jax.sharding import PartitionSpec as P

MESH = pl.DeviceIdType.MESH
REACT = 11
STEPS = 4
LEVELS = 4
C = 16
NZ = 128
T = 4
W = 2
E = T + 2 * W
DIRS = ((1, 1), (-1, -1), (1, -1), (-1, 1), (0, 1), (0, -1), (1, 0), (-1, 0))


def spans(d):
    if d == 1:
        return W + T - W, 0, W
    if d == -1:
        return W, W + T, W
    return W, W, T


def corner_spans(d):
    return (W + T - 1, W - 1, 1) if d == 1 else (W, W + T, 1)


def box(dx, dy):
    if dx and dy:
        return corner_spans(dx), corner_spans(dy)
    return spans(dx), spans(dy)


def here():
    lvl, gx, gy = lax.axis_index("lvl"), lax.axis_index("gx"), lax.axis_index("gy")
    y = gx % 4
    back = y // 2
    m = (y + back) % 2
    strip = 4 * (gx // 4) + m + (gy // 2) * (3 - 2 * m)
    return 2 * strip + gy % 2, lvl + back * (7 - 2 * lvl)


def device_at(X, Y):
    strip, back, r = X // 2, Y // 4, Y % 4
    s = strip % 4
    m = (s + s // 2) % 2
    y = m + back * (3 - 2 * m)
    return r + back * (3 - 2 * r), 4 * (strip // 4) + y, 2 * (s // 2) + X % 2


def kernel(nx, ny, ini, rf, d_ref, l_ref, quench_ref, formation_ref, out,
           stage, U, V2, V1, K, WX, WY, WZ, RHS, INV, ACC, INF, PQ, RF, flat, flat24,
           dh_ref, lr_ref, wq_ref, wf_ref, G,
           i_send, i_recv, u_send, u_recv, v_send, v_recv, g_send, g_recv, f_send, f_recv):
    lvl, gx, gy = lax.axis_index("lvl"), lax.axis_index("gx"), lax.axis_index("gy")
    me = (lvl, gx, gy)
    X, Y = here()

    def other(device):
        return (device[0] != lvl) | (device[1] != gx) | (device[2] != gy)

    def exists(dx, dy):
        ok = None
        for d, at, n in ((dx, X, nx), (dy, Y, ny)):
            if d:
                c = at < n - 1 if d == 1 else at > 0
                ok = c if ok is None else ok & c
        return ok

    beside = [(exists(dx, dy), device_at(X + dx, Y + dy)) for dx, dy in DIRS]
    gives = lvl // 2 == (gy + gy // 2) % 2
    YA = lvl + (gy // 2) * (7 - 2 * lvl)
    takers = [device_at(2 * gx + e, YA) for e in range(2)]
    giver = (lvl, X // 2, Y // 2)
    row_of_four = [((lvl + k) % LEVELS, gx, gy) for k in range(1, LEVELS)]

    def each(f):
        for i, (dx, dy) in enumerate(DIRS):
            @pl.when(beside[i][0])
            def _():
                f(i, dx, dy, beside[i][1])

    S0 = stage.at[1]
    zero = jnp.zeros((E, 24, NZ), jnp.float32)
    zero_v = jnp.zeros((E, C, NZ), jnp.float32)

    edge_x, edge_y = (X == 0) | (X == nx - 1), (Y == 0) | (Y == ny - 1)

    def clear(x, c):
        S0[x] = zero
        for p in range(LEVELS):
            V2[p, x] = zero_v
        return c

    @pl.when(edge_x | edge_y)
    def _():
        lax.fori_loop(0, E, clear, 0)

    bar = pltpu.get_barrier_semaphore()

    def greet(device):
        pl.semaphore_signal(bar, inc=1, device_id=device, device_id_type=MESH)

    each(lambda i, dx, dy, device: greet(device))
    others = [(lvl >= 0, device) for device in row_of_four]
    others += [(gives & other(device), device) for device in takers] + [(other(giver), giver)]
    for cond, device in others:
        @pl.when(cond)
        def _():
            greet(device)

    reacts = lax.broadcasted_iota(jnp.int32, (C, NZ), 0) < REACT
    dh_ref[...] = jnp.broadcast_to(0.5 * d_ref[...], (C, NZ))
    lr_ref[...] = jnp.where(reacts, jnp.broadcast_to(l_ref[...], (C, NZ)), 0.0)
    row, col = (lax.broadcasted_iota(jnp.int32, (4 * C, 4 * C), k) for k in range(2))
    for w_ref, m in ((wq_ref, quench_ref[...] * l_ref[...]), (wf_ref, formation_ref[...])):
        m = jnp.concatenate([jnp.concatenate([m] * 4, axis=1)] * 4, axis=0)
        m = jnp.where((row // C == col // C) & (row % C < REACT), m, 0.0)
        hi = m.astype(jnp.bfloat16).astype(jnp.float32)
        w_ref[...] = jnp.concatenate([hi, hi, m - hi], axis=1).astype(jnp.bfloat16)

    nat = stage.at[0]
    for x in range(8):
        nat[x, :, 0:C, :] = jnp.swapaxes(ini[:, x], 0, 1)
        nat[x, :, C:24, :] = jnp.broadcast_to(rf[x][:, None, :], (8, 8, NZ))

    count = sum(ok.astype(jnp.int32) for ok, _ in beside) + sum(cond.astype(jnp.int32) for cond, _ in others)
    pl.semaphore_wait(bar, count)

    def hand(e, device):
        return pltpu.make_async_remote_copy(
            src_ref=nat.at[T * e:T * e + T, pl.ds(T * (YA % 2), T)],
            dst_ref=S0.at[W:W + T, W:W + T],
            send_sem=i_send.at[1 + e], recv_sem=i_recv.at[1], device_id=device, device_id_type=MESH)

    for e, device in enumerate(takers):
        @pl.when(gives & other(device))
        def _():
            hand(e, device).start()

        @pl.when(gives & jnp.logical_not(other(device)))
        def _():
            for x in range(T):
                S0[W + x, W:W + T] = nat[T * e + x, pl.ds(T * (YA % 2), T)]

    @pl.when(other(giver))
    def _():
        hand(0, giver).wait_recv()

    def rim_copy(ref, send, recv, dx, dy, device):
        (sx, tx, mx), (sy, ty, my) = box(dx, dy)
        return pltpu.make_async_remote_copy(
            src_ref=ref.at[sx:sx + mx, sy:sy + my], dst_ref=ref.at[tx:tx + mx, ty:ty + my],
            send_sem=send, recv_sem=recv, device_id=device, device_id_type=MESH)

    inside = jnp.logical_not(edge_x | edge_y)
    at_corner = edge_x & edge_y
    at_edge = (edge_x | edge_y) & jnp.logical_not(at_corner)

    def rim_wait_for(ref, send, recv):
        for cond, cells in ((inside, 8 * W + 8 * W + 4), (at_edge, 12 * W + 2), (at_corner, 8 * W + 1)):
            @pl.when(cond)
            def _():
                copy = pltpu.make_async_remote_copy(
                    src_ref=ref.at[0:cells], dst_ref=ref.at[0:cells],
                    send_sem=send, recv_sem=recv, device_id=me, device_id_type=MESH)
                copy.wait_recv()
                copy.wait_send()

    each(lambda i, dx, dy, device: rim_copy(S0, i_send.at[0], i_recv.at[0], dx, dy, device).start())
    rim_wait_for(flat24, i_send.at[0], i_recv.at[0])
    for x in range(E):
        for h in range(2):
            RF[x, :, 8 * h:8 * h + 8, :] = S0[x, :, C:24, :]

    def rim_start(buf, send, recv, p):
        each(lambda i, dx, dy, device: rim_copy(buf.at[p], send.at[p], recv.at[p], dx, dy, device).start())

    def rim_wait(buf, send, recv, p):
        rim_wait_for(flat, send.at[p], recv.at[p])

    def back_copy(p, e, device):
        return pltpu.make_async_remote_copy(
            src_ref=U.at[p, W:W + T, W:W + T], dst_ref=G.at[p, pl.ds(T * e, T)],
            send_sem=g_send.at[p], recv_sem=g_recv.at[p, e], device_id=device, device_id_type=MESH)

    def back_start(p):
        @pl.when(other(giver))
        def _():
            back_copy(p, X % 2, giver).start()

        @pl.when(jnp.logical_not(other(giver)))
        def _():
            for x in range(T):
                G[p, T * (X % 2) + x] = U[p, W + x, W:W + T]

    def along_copy(p, e, source, YS):
        return pltpu.make_async_remote_copy(
            src_ref=G.at[p, T * e:T * e + T], dst_ref=out.at[T * e:T * e + T, pl.ds(T * (YS % 2), T)],
            send_sem=f_send.at[p, e], recv_sem=f_recv.at[source % 2, e], device_id=(p, gx, gy), device_id_type=MESH)

    def along_start(p, e):
        @pl.when(gives)
        def _():
            @pl.when(other(takers[e]))
            def _():
                back_copy(p, e, takers[e]).wait_recv()

            @pl.when(p != lvl)
            def _():
                along_copy(p, e, lvl, YA).start()

            @pl.when(p == lvl)
            def _():
                for x in range(T):
                    out[T * e + x, pl.ds(T * (YA % 2), T)] = G[p, T * e + x]

    lane = lax.broadcasted_iota(jnp.int32, (1, C, NZ), 2)
    first, last = lane == 0, lane == NZ - 1
    R = [(W, W + T) if x in (W - 1, W + T) else (W - 1, W + T + 1) for x in range(E)]

    def up(v):
        return pltpu.roll(v, 1, 2)

    def down(v):
        return pltpu.roll(v, NZ - 1, 2)

    def sweep(p, src, dst, rows, cols):
        for x in rows:
            lo, hi = cols(x)
            for a in range(lo, hi, 2):
                b = min(a + 2, hi)
                c = src(x, a - 1, b + 1)
                v, wz = c[1:-1], WZ[p, x, a:b]
                wy = WY[p, x, a - 1:b]
                n = (WX[p, x - 1, a:b] * src(x - 1, a, b) + WX[p, x, a:b] * src(x + 1, a, b)
                     + wy[:-1] * c[:-2] + wy[1:] * c[2:] + wz * up(v) + down(wz * v))
                dst(x, a, b, (RHS[p, x, a:b] + n) * INV[p, x, a:b])

    def split(u):
        hi = u.astype(jnp.bfloat16)
        lo = (u - hi.astype(jnp.float32)).astype(jnp.bfloat16)
        return jnp.concatenate([hi, lo, hi], axis=0)

    def chemistry(p, own):
        def one(get, put):
            u = get().reshape(4 * C, NZ)
            for k, w_ref, v in ((0, wf_ref, u), (1, wq_ref, u * u)):
                put(k, jnp.dot(w_ref[...], split(v), preferred_element_type=jnp.float32).reshape(4, C, NZ))

        for x in range(W, W + T) if own else (W - 1, W + T):
            def put(k, v, x=x):
                PQ[k, x, W:W + T] = v
            one(lambda: U[p, x, W:W + T], put)
        for y in () if own else (W - 1, W + T):
            def put(k, v, y=y):
                for x in range(T):
                    PQ[k, W + x, y] = v[x]
            one(lambda: U[p, W:W + T, y], put)

    def setup(p):
        dh = dh_ref[...][None]
        lr = lr_ref[...][None]
        for x in range(E):
            lo, hi = (W, W + T) if x in (0, E - 1) else (R[x] if x in (1, E - 2) else (0, E))
            if x in (1, E - 2):
                lo, hi = 1, E - 1
            for a in range(lo, hi, 2):
                u = U[p, x, a:a + 2]
                K[x, a:a + 2] = dh + dh * (u * u)
        chemistry(p, False)
        for x in range(W - 1, W + T + 1):
            lo, hi = R[x]
            for a in range(lo, hi, hi - lo):
                b = hi
                kc = K[x, a - 1:b + 1]
                k = kc[1:-1]
                kw, ke = K[x - 1, a:b], K[x + 1, a:b]
                ww, we, ws, wn = k + kw, k + ke, k + kc[:-2], k + kc[2:]
                kl = jnp.where(first, dh, up(k))
                kh = jnp.where(last, dh, down(k))
                wl = k + kl
                total = ((ww + we) + (ws + wn)) + (wl + (k + kh))
                wz = jnp.where(first, 0.0, wl)
                if x <= W + T - 1:
                    WX[p, x - 1, a:b] = ww
                if x >= W + T - 1:
                    WX[p, x, a:b] = we
                WY[p, x, a - 1:b - 1] = ws
                if b == hi:
                    WY[p, x, b - 1:b] = wn[-1:]
                WZ[p, x, a:b] = wz
                uc = U[p, x, a - 1:b + 1]
                u = uc[1:-1]
                n = (ww * U[p, x - 1, a:b] + we * U[p, x + 1, a:b] + ws * uc[:-2] + wn * uc[2:]
                     + wz * up(u) + down(wz * u))
                r = RF[x, a:b]
                made = r * PQ[0, x, a:b]
                lost = total + r * (lr + PQ[1, x, a:b])
                half = 0.5 * ((n + made) - lost * u)
                inv = 1.0 / (1.0 + lost)
                inflow = INF[x, a:b]
                old = ACC[p, x, a:b]
                right = (u + made) + inflow
                INF[x, a:b] = (old + half) - u
                ACC[p, x, a:b] = (half + u) + inflow
                RHS[p, x, a:b] = right
                INV[p, x, a:b] = inv
                V1[x, a:b] = (right + n) * inv

    none_v = jnp.zeros((1, C, NZ), jnp.float32)

    def mask(p):
        for cond, cells in ((X == 0, [(W - 1, y) for y in range(W, W + T)]),
                            (X == nx - 1, [(W + T, y) for y in range(W, W + T)]),
                            (Y == 0, [(x, W - 1) for x in range(W, W + T)]),
                            (Y == ny - 1, [(x, W + T) for x in range(W, W + T)])):
            @pl.when(cond)
            def _():
                for x, y in cells:
                    V1[x, y:y + 1] = none_v
                    INV[p, x, y:y + 1] = none_v

    inner = range(W, W + T)
    outer = range(W - 1, W + T + 1)

    def store_v1(x, a, b, v):
        V1[x, a:b] = v

    def phase_a(t, p):
        n = t - p

        @pl.when((n >= 0) & ((n < STEPS) | ((n == STEPS) & (p < LEVELS - 1))))
        def _():
            @pl.when(n == 0)
            def _():
                for x in range(E):
                    U[p, x] = S0[x, :, 0:C, :]

            chemistry(p, True)

            @pl.when(n > 0)
            def _():
                rim_wait(U, u_send, u_recv, p)

            setup(p)

            @pl.when(n < STEPS)
            def _():
                mask(p)

                def put(x, a, b, v):
                    V2[p, x, a:b] = v
                sweep(p, lambda x, a, b: V1[x, a:b], put, inner, lambda x: (W, W + T))
                rim_start(V2, v_send, v_recv, p)

    def phase_b(t, p):
        n = t - p

        @pl.when((n >= 0) & (n < STEPS))
        def _():
            rim_wait(V2, v_send, v_recv, p)
            sweep(p, lambda x, a, b: V2[p, x, a:b], store_v1, outer, lambda x: R[x])

            def put(x, a, b, v):
                U[p, x, a:b] = v
            sweep(p, lambda x, a, b: V1[x, a:b], put, inner, lambda x: (W, W + T))

            @pl.when((n < STEPS - 1) | (p < LEVELS - 1))
            def _():
                rim_start(U, u_send, u_recv, p)

            @pl.when(n == STEPS - 1)
            def _():
                back_start(p)

    def tick(t, c):
        for x in range(1, E - 1):
            INF[x] = zero_v
        lax.fori_loop(0, LEVELS, lambda p, c: (phase_a(t, p), c)[1], 0)

        @pl.when(t >= LEVELS)
        def _():
            along_start(t - LEVELS, 0)

        lax.fori_loop(0, LEVELS, lambda p, c: (phase_b(t, p), c)[1], 0)

        @pl.when(t >= LEVELS)
        def _():
            along_start(t - LEVELS, 1)

        return c

    lax.fori_loop(0, STEPS + LEVELS - 1, tick, 0)

    for e in range(2):
        along_start(LEVELS - 1, e)

    first_source = 2 * ((gy + gy // 2) % 2)
    for k in range(2):
        source = first_source + k

        @pl.when(source != lvl)
        def _():
            for e in range(2):
                along_copy(lvl, e, source, source + (gy // 2) * (7 - 2 * source)).wait_recv()
    for p in range(LEVELS):
        @pl.when(other(giver))
        def _():
            back_copy(p, X % 2, giver).wait_send()

        @pl.when(gives & (p != lvl))
        def _():
            for e in range(2):
                along_copy(p, e, lvl, YA).wait_send()

    for e, device in enumerate(takers):
        @pl.when(gives & other(device))
        def _():
            hand(e, device).wait_send()


def on_device(nx, ny, initial, rate_factor, diffusivity, loss_rate, quench, formation):
    f32 = jnp.float32
    frame = (E, E, C, NZ)
    vmem = pl.BlockSpec(memory_space=pltpu.VMEM)
    dma = pltpu.SemaphoreType.DMA
    done = pl.pallas_call(
        functools.partial(kernel, nx, ny),
        name="deferred_correction",
        out_shape=jax.ShapeDtypeStruct((8, 8, C, NZ), f32),
        in_specs=[vmem] * 6,
        out_specs=vmem,
        scratch_shapes=[
            pltpu.VMEM((2, E, E, 24, NZ), f32),
            pltpu.VMEM((LEVELS,) + frame, f32),
            pltpu.VMEM((LEVELS,) + frame, f32),
            pltpu.VMEM(frame, f32),
            pltpu.VMEM(frame, f32),
            pltpu.VMEM((LEVELS,) + frame, f32),
            pltpu.VMEM((LEVELS,) + frame, f32),
            pltpu.VMEM((LEVELS,) + frame, f32),
            pltpu.VMEM((LEVELS,) + frame, f32),
            pltpu.VMEM((LEVELS,) + frame, f32),
            pltpu.VMEM((LEVELS,) + frame, f32),
            pltpu.VMEM(frame, f32),
            pltpu.VMEM((2,) + frame, f32),
            pltpu.VMEM(frame, f32),
            pltpu.VMEM((16 * W + 4, C, NZ), f32),
            pltpu.VMEM((16 * W + 4, 24, NZ), f32),
            pltpu.VMEM((C, NZ), f32), pltpu.VMEM((C, NZ), f32),
            pltpu.VMEM((4 * C, 12 * C), jnp.bfloat16), pltpu.VMEM((4 * C, 12 * C), jnp.bfloat16),
            pltpu.VMEM((LEVELS, 2 * T, T, C, NZ), f32),
            dma((3,)), dma((2,)),
            dma((LEVELS,)), dma((LEVELS,)),
            dma((LEVELS,)), dma((LEVELS,)),
            dma((LEVELS,)), dma((LEVELS, 2)),
            dma((LEVELS, 2)), dma((2, 2)),
        ],
        compiler_params=pltpu.CompilerParams(
            collective_id=0, has_side_effects=True, vmem_limit_bytes=44 << 20),
    )(initial, rate_factor, diffusivity[:, None], loss_rate[:, None], quench, formation)
    return done.transpose(2, 0, 1, 3)[None]


def solution(mesh):
    in_specs = (P(None, "gx", "gy", None), P("gx", "gy", None), P(), P(), P(), P())
    out_specs = P("lvl", None, "gx", "gy", None)
    nx, ny = 2 * mesh.shape["gx"], 2 * mesh.shape["gy"]
    return jax.shard_map(
        functools.partial(on_device, nx, ny), mesh=mesh, in_specs=in_specs, out_specs=out_specs, check_vma=False)
```
